256 devices in a mesh: region: 8 (over x, core), sub: 32 (over y, z).
Axes of the slice: x: 4, y: 4, z: 8, core: 2. Of those that a mesh axis runs over, the one named last changes fastest.
Arguments:
- multipliers: float32 [256, 3, 3, 256], P(('region', 'sub')), may hold values from -6 to 6
- direction: float32 [256, 3, 3, 256], P(('region', 'sub')), may hold values from -12 to 12
- residual: float32 [256, 3, 3, 256], P(('region', 'sub')), may hold values from -12 to 12
- reaction: float32 [256, 16, 256], P(('region', 'sub')), may hold values from 0.1 to 2
- viscosity: float32 [256, 16, 256], P(('region', 'sub')), may hold values from 0.5 to 5
- primal_index: int32 [256, 96], P(('region', 'sub')), may hold values from 17 to 2286, as said below
- region_inverse: float32 [8, 3072, 3072], P('region', 'sub'), as said below
- coarse_map: float32 [256, 96, 384], P(('region', 'sub')), may hold values from -0.4375 to 0.4375
- global_inverse: float32 [384, 384], replicated, as said below
Outputs:
- new_multipliers: float32 [256, 3, 3, 256], P(('region', 'sub'))
- new_residual: float32 [256, 3, 3, 256], P(('region', 'sub'))
- velocity: float32 [256, 3, 16, 256], P(('region', 'sub'))
- pressure: float32 [256, 16, 256], P(('region', 'sub'))
The draws below stay inside these ranges and needn't reach their ends.
Inputs may be any that keep to these rules, and one draw needn't show every extreme that they name: `primal_index`: each row holds 96 different positions, each in the interior of a face (neither face index 0 nor 16 - 1); every row contains the first such position and the last one. `region_inverse`: each region's matrix is symmetric positive definite. `global_inverse`: symmetric positive definite.
All inputs are finite; a program needn't handle non-finite values.
Results may differ from the reference program's by a relative error of at most 0.0001.
Values sent between devices are 32-bit elements; how exact they have to be, the bound alone decides.
A program may use at most 64 MiB of HBM per device.

```python
import math
import jax
import jax.numpy as jnp
from jax import lax

CELLS = 16
DOM_Z = 4
PRIMAL = 96
GLOBAL_DOFS = 384
LEVELS = 3
SWEEPS = 1
COARSE_SWEEPS = 8
VCYCLES = 2
DOMAINS = 256
FACE = 256
REGION_DOFS = 3072
N_REGION = 8
N_SUB = 32


def face_values(key):
    shape = (DOMAINS, 3, 3, FACE)
    position = jnp.arange(DOMAINS, dtype=jnp.float32) / max(DOMAINS - 1, 1)
    values = jnp.clip(jax.random.normal(key, shape, jnp.float32), -4.0, 4.0)
    growth = 1.0 + 2.0 * position
    return values * growth[:, None, None, None]


def draw_direction(key, part):
    return face_values(jax.random.fold_in(key, 11))


def draw_residual(key, part):
    return face_values(jax.random.fold_in(key, 13))


def draw_primal_index(key, part):
    inner = CELLS - 2
    count = 9 * inner * inner
    keys = jax.random.split(jax.random.fold_in(key, 23), DOMAINS)

    def one_row(subkey):
        middle = jax.random.permutation(subkey, count - 2)[:PRIMAL - 2].astype(jnp.int32) + 1
        order = jnp.concatenate([jnp.zeros((1,), jnp.int32), middle, jnp.full((1,), count - 1, jnp.int32)])
        block = order // (inner * inner)
        rest = order % (inner * inner)
        return block * (CELLS * CELLS) + (rest // inner + 1) * CELLS + rest % inner + 1
    return jax.vmap(one_row)(keys)


def spd_matrix(key, order):
    factor = jax.random.normal(key, (order, order), jnp.float32) / jnp.sqrt(jnp.float32(order))
    product = jnp.dot(factor, factor.T, precision=lax.Precision.HIGHEST)
    return 0.5 * (product + product.T) + 0.5 * jnp.eye(order, dtype=jnp.float32)


def draw_region_inverse(key, part):
    keys = jax.random.split(jax.random.fold_in(key, 31), N_REGION)
    return jax.vmap(lambda subkey: spd_matrix(subkey, REGION_DOFS))(keys)


def draw_global_inverse(key, part):
    return spd_matrix(jax.random.fold_in(key, 37), GLOBAL_DOFS)


def with_spikes(values, own_key, source, target, blocks, factor):
    def block_of(dim):
        return (jnp.arange(values.shape[dim]) // (values.shape[dim] // blocks)).reshape((-1,) + (1,) * (values.ndim - 1 - dim))

    one_side = jax.random.permutation(own_key, blocks)[block_of(target)]
    second = (block_of(target) + blocks // 2) % blocks
    return jnp.where((block_of(source) == one_side) | (block_of(source) == second), factor * values, values)


def steps_of(stream_key, dims, cuts, low, largest):
    loudness, own = 1.0, jax.random.fold_in(stream_key, 6)
    for dim, blocks in cuts:
        heights = jnp.exp(jax.random.uniform(jax.random.fold_in(own, dim), (blocks,), jnp.float32, low / len(cuts), largest / len(cuts)))
        loudness = loudness * jnp.repeat(heights, dims[dim] // blocks).reshape([-1 if axis == dim else 1 for axis in range(len(dims))])
    return loudness


def noise(own_key, dims, width, bound, shards=(), kind=jnp.bfloat16):
    result = width * jax.random.normal(own_key, dims, jnp.float32)
    if shards:
        result = result * steps_of(own_key, dims, shards, -0.22, 0.18)
    return jnp.clip(result, -bound, bound).astype(kind)


def bell_draw_with(rng, shape, scale, bound, cuts, heavy, held_as=jnp.bfloat16):
    values = scale * jax.random.normal(rng, shape, jnp.float32)
    if cuts:
        values = values * steps_of(rng, shape, cuts, -0.22, 0.18)
    return jnp.clip(with_spikes(values, jax.random.fold_in(rng, 3), *heavy), -bound, bound).astype(held_as)


def setup_inputs(seed: int = 0) -> dict:
    streams_of = jax.random.split(jax.random.key(seed), 10)
    multipliers = noise(streams_of[0], (DOMAINS, 3, 3, FACE), 1.0, 6.0, ((0, 256),), jnp.float32)
    direction = draw_direction(jax.random.fold_in(streams_of[9], 71), 0)
    residual = draw_residual(jax.random.fold_in(streams_of[9], 71), 0)
    reaction = jnp.clip(jnp.exp(math.log(2.0) - 2.9957323 * jax.random.uniform(streams_of[3], (DOMAINS, CELLS, FACE), jnp.float32) ** steps_of(streams_of[3], (DOMAINS, CELLS, FACE), ((0, 256),), -0.2, 0.2)), 0.1, 2.0)
    viscosity = jnp.clip(jnp.exp(math.log(5.0) - 2.3025851 * jax.random.uniform(streams_of[4], (DOMAINS, CELLS, FACE), jnp.float32) ** steps_of(streams_of[4], (DOMAINS, CELLS, FACE), ((0, 256),), -0.2, 0.2)), 0.5, 5.0)
    primal_index = draw_primal_index(jax.random.fold_in(streams_of[9], 71), 0)
    region_inverse = draw_region_inverse(jax.random.fold_in(streams_of[9], 71), 0)
    coarse_map = bell_draw_with(streams_of[7], (DOMAINS, PRIMAL, GLOBAL_DOFS), REGION_DOFS ** -0.5, 0.4375, ((0, 256),), (0, 2, 128, 5.5), jnp.float32)
    global_inverse = draw_global_inverse(jax.random.fold_in(streams_of[9], 71), 0)
    return dict(multipliers=multipliers, direction=direction, residual=residual, reaction=reaction, viscosity=viscosity, primal_index=primal_index, region_inverse=region_inverse, coarse_map=coarse_map, global_inverse=global_inverse)


damping = 0.8


def operate(field, react, weight):
    padded = jnp.pad(field, ((0, 0), (1, 1), (1, 1), (1, 1)))
    beside = padded[:, 2:, 1:-1, 1:-1] + padded[:, :-2, 1:-1, 1:-1]
    beside = beside + padded[:, 1:-1, 2:, 1:-1] + padded[:, 1:-1, :-2, 1:-1]
    beside = beside + padded[:, 1:-1, 1:-1, 2:] + padded[:, 1:-1, 1:-1, :-2]
    return react * field + weight * (6.0 * field - beside)


def restrict(array):
    shape = array.shape
    lead = shape[:-3]
    return array.reshape(lead + (shape[-3] // 2, 2, shape[-2] // 2, 2, shape[-1] // 2, 2)).mean(axis=(-5, -3, -1))


def prolong(array):
    return jnp.repeat(jnp.repeat(jnp.repeat(array, 2, axis=-3), 2, axis=-2), 2, axis=-1)


def relax(field, source, react, weight, count):
    diagonal = react + 6.0 * weight
    for _ in range(count):
        field = field + damping * (source - operate(field, react, weight)) / diagonal
    return field


def vcycle(field, source, reacts, level):
    weight = 0.25 ** level
    if level == LEVELS - 1:
        return relax(field, source, reacts[level], weight, COARSE_SWEEPS)
    field = relax(field, source, reacts[level], weight, SWEEPS)
    remain = restrict(source - operate(field, reacts[level], weight))
    coarse = vcycle(jnp.zeros_like(remain), remain, reacts, level + 1)
    field = field + prolong(coarse)
    return relax(field, source, reacts[level], weight, SWEEPS)


def local_solve(source, react):
    reacts = [react]
    for _ in range(LEVELS - 1):
        reacts.append(restrict(reacts[-1]))
    field = jnp.zeros_like(source)
    for _ in range(VCYCLES):
        field = vcycle(field, source, reacts, 0)
    return field


def face_cells(picked):
    face = CELLS * CELLS
    block = picked // (3 * face)
    component = (picked // face) % 3
    spot = picked % face
    first = spot // CELLS
    second = spot % CELLS
    upper = CELLS - 1
    place = jnp.where(block == 0, upper * face + spot, jnp.where(block == 1, first * face + upper * CELLS + second, first * face + second * CELLS + upper))
    return component * (CELLS * face) + place


def reference(multipliers, direction, residual, reaction, viscosity, primal_index, region_inverse, coarse_map, global_inverse):
    highest = lax.Precision.HIGHEST
    face = CELLS * CELLS
    rows_y = N_SUB // DOM_Z
    active = direction
    grid = active.reshape(N_REGION, rows_y, DOM_Z, 3, 3, face)
    below_x = jnp.roll(grid[:, :, :, 0], 1, axis=0)
    below_y = jnp.roll(grid[:, :, :, 1], 1, axis=1)
    below_z = jnp.roll(active.reshape(N_REGION, N_SUB, 3, 3, face)[:, :, 2], 1, axis=1).reshape(N_REGION, rows_y, DOM_Z, 3, face)
    below = jnp.stack([below_x, below_y, below_z], axis=3).reshape(DOMAINS, 3, 3, face)
    reacts = reaction.reshape(DOMAINS, CELLS, CELLS, CELLS)

    def one_domain(pieces):
        own, under, react = pieces
        cubic = (3, CELLS, CELLS)
        source = jnp.zeros((3, CELLS, CELLS, CELLS), jnp.float32)
        source = source.at[:, CELLS - 1, :, :].add(own[0].reshape(cubic))
        source = source.at[:, :, CELLS - 1, :].add(own[1].reshape(cubic))
        source = source.at[:, :, :, CELLS - 1].add(own[2].reshape(cubic))
        source = source.at[:, 0, :, :].add(-under[0].reshape(cubic))
        source = source.at[:, :, 0, :].add(-under[1].reshape(cubic))
        source = source.at[:, :, :, 0].add(-under[2].reshape(cubic))
        return local_solve(source, react)

    base = lax.map(one_domain, (active, below, reacts))
    primal = jnp.take_along_axis(active.reshape(DOMAINS, -1), primal_index, axis=1)
    grouped = primal.reshape(N_REGION, REGION_DOFS)
    region_part = jnp.einsum("rij,rj->ri", region_inverse, grouped, precision=highest).reshape(DOMAINS, PRIMAL)
    total = jnp.einsum("skg,sk->g", coarse_map, primal, precision=highest)
    top = jnp.dot(global_inverse, total, precision=highest)
    lifted = region_part + jnp.einsum("skg,g->sk", coarse_map, top, precision=highest)
    spots = face_cells(primal_index)
    flat = base.reshape(DOMAINS, -1)
    flat = jax.vmap(lambda row, where_to, values: row.at[where_to].add(values))(flat, spots, lifted)
    fields = flat.reshape(DOMAINS, 3, CELLS, CELLS, CELLS)
    upper = jnp.stack([fields[:, :, CELLS - 1, :, :], fields[:, :, :, CELLS - 1, :], fields[:, :, :, :, CELLS - 1]], axis=1).reshape(DOMAINS, 3, 3, face)
    lower_flat = jnp.stack([fields[:, :, 0, :, :], fields[:, :, :, 0, :], fields[:, :, :, :, 0]], axis=1).reshape(DOMAINS, 3, 3, face)
    lower = lower_flat.reshape(N_REGION, rows_y, DOM_Z, 3, 3, face)
    after_x = jnp.roll(lower[:, :, :, 0], -1, axis=0)
    after_y = jnp.roll(lower[:, :, :, 1], -1, axis=1)
    after_z = jnp.roll(lower_flat.reshape(N_REGION, N_SUB, 3, 3, face)[:, :, 2], -1, axis=1).reshape(N_REGION, rows_y, DOM_Z, 3, face)
    after = jnp.stack([after_x, after_y, after_z], axis=3).reshape(DOMAINS, 3, 3, face)
    jump = upper - after
    views = viscosity.reshape(DOMAINS, CELLS, CELLS, CELLS)

    def pressure_one(pieces):
        field, ahead, visc = pieces
        step_x = jnp.concatenate([field[0, 1:], ahead[0, 0].reshape(1, CELLS, CELLS)], axis=0) - field[0]
        step_y = jnp.concatenate([field[1, :, 1:], ahead[1, 1].reshape(CELLS, 1, CELLS)], axis=1) - field[1]
        step_z = jnp.concatenate([field[2, :, :, 1:], ahead[2, 2].reshape(CELLS, CELLS, 1)], axis=2) - field[2]
        return -visc * (step_x + step_y + step_z)

    pressure = lax.map(pressure_one, (fields, after, views)).reshape(DOMAINS, CELLS, face)
    velocity = fields.reshape(DOMAINS, 3, CELLS, face)
    curvature = jnp.sum(active * jump)
    squares = jnp.sum(residual * residual)
    alpha = squares / curvature
    return (multipliers + alpha * active, residual - alpha * jump, velocity, pressure)
```

```python
import functools

import jax
import jax.numpy as jnp
from jax import lax
from jax.experimental import pallas as pl
from jax.experimental.pallas import tpu as pltpu
from jax.sharding import PartitionSpec as P

DOM_Z = 4
COARSE_SWEEPS = 8
CELLS = 16
FACE = 256
DAMPING = 0.8
KEEP = 0.2
MESH = pl.DeviceIdType.MESH
F32 = jnp.float32
BF16 = jnp.bfloat16


def iota(shape, axis):
    return lax.broadcasted_iota(jnp.int32, shape, axis)


def split(field):
    lead = field.shape[0] // CELLS
    cubic = field.reshape(lead, CELLS, FACE)
    return [cubic[:, 8 * i : 8 * i + 8, 128 * j : 128 * j + 128] for i in (0, 1) for j in (0, 1)]


def join(parts):
    low = jnp.concatenate([parts[0], parts[1]], axis=2)
    high = jnp.concatenate([parts[2], parts[3]], axis=2)
    whole = jnp.concatenate([low, high], axis=1)
    return whole.reshape(whole.shape[0] * CELLS, FACE)


def neighbours(parts, step):
    shape = parts[0].shape
    x = iota(shape, 1)
    lane = iota(shape, 2)
    y = lane >> 4
    z = lane & 15

    def roll(v, by, axis):
        return pltpu.roll(v, by % v.shape[axis], axis)

    sums = []
    ys_up = [roll(v, 16 * step, 2) for v in parts]
    ys_down = ys_up if step == 4 else [roll(v, -16 * step, 2) for v in parts]
    xs_up = [roll(v, step, 1) for v in parts]
    xs_down = xs_up if step == 4 else [roll(v, -step, 1) for v in parts]
    for i in (0, 1):
        for j in (0, 1):
            k = 2 * i + j
            v = parts[k]
            total = jnp.where(z >= step, roll(v, step, 2), 0.0)
            total = total + jnp.where(z < CELLS - step, roll(v, -step, 2), 0.0)
            before = ys_up[k - 1] if j == 1 else 0.0
            total = total + jnp.where(y >= step, ys_up[k], before)
            after = ys_down[k + 1] if j == 0 else 0.0
            total = total + jnp.where(y < 8 - step, ys_down[k], after)
            before = xs_up[k - 2] if i == 1 else 0.0
            total = total + jnp.where(x >= step, xs_up[k], before)
            after = xs_down[k + 2] if i == 0 else 0.0
            total = total + jnp.where(x < 8 - step, xs_down[k], after)
            sums.append(total)
    return sums


def block_mean(parts, step):
    shape = parts[0].shape
    x = iota(shape, 1)
    lane = iota(shape, 2)

    def pair(v, by, axis, even):
        count = v.shape[axis]
        return v + jnp.where(even, pltpu.roll(v, count - by, axis), pltpu.roll(v, by, axis))

    result = []
    for v in parts:
        v = pair(v, step, 2, (lane & step) == 0)
        v = pair(v, 16 * step, 2, ((lane >> 4) & step) == 0)
        v = pair(v, step, 1, (x & step) == 0)
        result.append(v * 0.125)
    return result


def merge(parts):
    spot = iota(parts[0].shape[1:], 1) & 3
    return [jnp.where(spot == 0, v[0], jnp.where(spot == 1, v[1], v[2]))[None] for v in parts]


def unmerge(parts):
    result = []
    for v in parts:
        v = v[0]
        spot = iota(v.shape, 1) & 3
        moved = {by: pltpu.roll(v, by % 128, 1) if by else v for by in range(-2, 4)}
        comps = []
        for c in range(3):
            value = moved[3 - c]
            for t in (2, 1, 0):
                value = jnp.where(spot == t, moved[t - c], value)
            comps.append(value)
        result.append(jnp.stack(comps, axis=0))
    return result


def broad(parts):
    return [jnp.broadcast_to(v, (3,) + v.shape[1:]) for v in parts]


def coarse_solve(source, scale2):
    b = merge(source)
    wb = [w * s for w, s in zip(scale2, b)]
    v = wb
    for _ in range(COARSE_SWEEPS - 1):
        near = neighbours(v, 4)
        v = [KEEP * a + (c + (w * 0.0625) * n) for a, c, w, n in zip(v, wb, scale2, near)]
    return unmerge(v)


def middle_solve(source, scale1, scale2):
    wb = [w * s for w, s in zip(scale1, source)]
    near = neighbours(wb, 2)
    remain = [KEEP * s + 0.25 * n for s, n in zip(source, near)]
    coarse = coarse_solve(block_mean(remain, 2), scale2)
    v = [a + c for a, c in zip(wb, coarse)]
    near = neighbours(v, 2)
    return [KEEP * a + (c + (w * 0.25) * n) for a, c, w, n in zip(v, wb, scale1, near)]


def local_solve(source, diag0, scale0, scale1, scale2):
    wb = [w * s for w, s in zip(scale0, source)]
    v = None
    for cycle in range(2):
        if cycle == 0:
            v = wb
            remain = [KEEP * s + n for s, n in zip(source, neighbours(v, 1))]
        else:
            near = neighbours(v, 1)
            v = [KEEP * a + (c + w * n) for a, c, w, n in zip(v, wb, scale0, near)]
            near = neighbours(v, 1)
            remain = [(s - d * a) + n for s, d, a, n in zip(source, diag0, v, near)]
        coarse = middle_solve(block_mean(remain, 1), scale1, scale2)
        v = [a + c for a, c in zip(v, coarse)]
        near = neighbours(v, 1)
        v = [KEEP * a + (c + w * n) for a, c, w, n in zip(v, wb, scale0, near)]
    return v


def exact_dot(left, right):
    high = left.astype(BF16)
    rest = left - high.astype(F32)
    mid = rest.astype(BF16)
    low = (rest - mid.astype(F32)).astype(BF16)
    dot = functools.partial(jnp.dot, preferred_element_type=F32)
    return dot(high, right) + (dot(mid, right) + dot(low, right))


def spread(rows):
    own = (iota((CELLS, FACE), 1) >> 4) == iota((CELLS, FACE), 0)
    return jnp.concatenate([jnp.where(own, jnp.broadcast_to(r, (CELLS, FACE)), 0.0) for r in rows], axis=0)


def collect(field):
    own = (iota((CELLS, FACE), 1) >> 4) == iota((CELLS, FACE), 0)
    return [
        jnp.sum(jnp.where(own, field[CELLS * c : CELLS * c + CELLS], 0.0), axis=0, keepdims=True)
        for c in range(3)
    ]


def kernel(
    n_region,
    n_sub,
    multipliers,
    direction,
    residual,
    reaction,
    viscosity,
    primal_index,
    region_inverse,
    coarse_map,
    global_inverse,
    new_multipliers,
    new_residual,
    velocity,
    pressure,
    v_mult,
    v_dir,
    v_res,
    v_react,
    v_visc,
    v_index,
    v_rows,
    v_map,
    v_ginv,
    table,
    padded_index,
    halo,
    face_send,
    after,
    packet,
    gather,
    packet2,
    gather2,
    packet3,
    gather3,
    packet4,
    gather4,
    load_sem,
    halo_send,
    halo_recv,
    back_send,
    back_recv,
    sum_send,
    sum_recv,
):
    region = lax.axis_index("region")
    sub = lax.axis_index("sub")

    def sub_peer(i):
        return (region, lax.rem(sub + i, n_sub))

    def region_peer(i):
        return (lax.rem(region + i, n_region), sub)

    loads = [
        pltpu.make_async_copy(src, dst, load_sem.at[i])
        for i, (src, dst) in enumerate(
            (
                (direction, v_dir),
                (primal_index, v_index),
                (coarse_map, v_map),
                (residual, v_res),
                (reaction, v_react),
                (region_inverse, v_rows),
                (global_inverse, v_ginv),
                (multipliers, v_mult),
                (viscosity, v_visc),
            )
        )
    ]
    for load in loads:
        load.start()

    barrier = pltpu.get_barrier_semaphore()

    def greet_sub(i, carry):
        pl.semaphore_signal(barrier, inc=1, device_id=sub_peer(i), device_id_type=MESH)
        return carry

    def greet_region(i, carry):
        pl.semaphore_signal(barrier, inc=1, device_id=region_peer(i), device_id_type=MESH)
        return carry

    lax.fori_loop(1, n_sub, greet_sub, 0)
    lax.fori_loop(1, n_region, greet_region, 0)

    def send_all(src, dst_of_me, count, peer, index):
        def one(i, carry):
            pltpu.make_async_remote_copy(
                src_ref=src,
                dst_ref=dst_of_me,
                send_sem=sum_send.at[index],
                recv_sem=sum_recv.at[index],
                device_id=peer(i),
                device_id_type=MESH,
            ).start()
            return carry

        lax.fori_loop(1, count, one, 0)

    def all_of(buffer, count, peer, index):
        part = buffer.at[pl.ds(0, count - 1)]
        return pltpu.make_async_remote_copy(
            src_ref=part,
            dst_ref=part,
            send_sem=sum_send.at[index],
            recv_sem=sum_recv.at[index],
            device_id=peer(1),
            device_id_type=MESH,
        )

    row_i = iota((FACE, FACE), 0)
    col_i = iota((FACE, FACE), 1)
    table[0] = jnp.where((row_i & 15) == (col_i & 15), 1.0, 0.0).astype(BF16)
    table[1] = jnp.where((row_i & 15) == (col_i >> 4), 1.0, 0.0).astype(BF16)
    table[2] = jnp.where((row_i >> 4) == (col_i & 15), 1.0, 0.0).astype(BF16)

    loads[0].wait()
    loads[1].wait()
    padded_index[...] = jnp.full((8, 128), -1, jnp.int32)
    padded_index[0:1, 0:96] = v_index[...]
    index_row = padded_index[0:1, :]
    index_col = jnp.transpose(jnp.broadcast_to(index_row.astype(F32), (128, 128))).astype(jnp.int32)
    lane128 = iota((128, 128), 1)
    hit = jnp.where((index_col & 127) == lane128, 1.0, 0.0)
    key_col = index_col >> 7
    picked = jnp.zeros((128, 128), F32)
    for d in range(3):
        for c in range(3):
            for h in range(2):
                r = (d * 3 + c) * 2 + h
                values = v_dir[0, d, c : c + 1, 128 * h : 128 * h + 128]
                picked = jnp.where(key_col == r, jnp.broadcast_to(values, (128, 128)), picked)
    picked = picked * hit
    primal_row = jnp.sum(jnp.transpose(picked), axis=0, keepdims=True)
    primal_col = jnp.sum(picked, axis=1, keepdims=True)[:96]
    loads[2].wait()
    share = jnp.sum(primal_col * v_map[0], axis=0, keepdims=True)
    loads[3].wait()
    squares = jnp.sum(v_res[0] * v_res[0])
    lane_row = iota((1, 128), 1)
    packet[0:1, :] = jnp.where(lane_row < 96, primal_row, squares)
    for j in range(3):
        packet[j + 1 : j + 2, :] = share[:, 128 * j : 128 * j + 128]
    gather[sub] = packet[...]

    pl.semaphore_wait(barrier, n_sub - 1 + n_region - 1)

    above = (region_peer(1), sub_peer(DOM_Z), sub_peer(1))
    below = (region_peer(n_region - 1), sub_peer(n_sub - DOM_Z), sub_peer(n_sub - 1))
    faces = [
        pltpu.make_async_remote_copy(
            src_ref=v_dir.at[0, d],
            dst_ref=halo.at[d],
            send_sem=halo_send.at[d],
            recv_sem=halo_recv.at[d],
            device_id=above[d],
            device_id_type=MESH,
        )
        for d in (1, 2, 0)
    ]
    for copy in faces:
        copy.start()
    send_all(packet, gather.at[sub], n_sub, sub_peer, 0)

    lane = iota((CELLS, FACE), 1)
    y_lane = lane >> 4
    z_lane = lane & 15
    x_row = iota((CELLS, FACE), 0)
    same, to_z, from_z = 0, 1, 2

    def tile3(mask):
        return jnp.concatenate([mask] * 3, axis=0)

    def natural(face_rows, edge):
        in_y = exact_dot(spread(face_rows[1]), table[same])
        in_z = exact_dot(spread(face_rows[2]), table[to_z])
        blocks = []
        for c in range(3):
            part = jnp.where(x_row == edge, jnp.broadcast_to(face_rows[0][c], (CELLS, FACE)), 0.0)
            part = part + jnp.where(y_lane == edge, in_y[CELLS * c : CELLS * c + CELLS], 0.0)
            part = part + jnp.where(z_lane == edge, in_z[CELLS * c : CELLS * c + CELLS], 0.0)
            blocks.append(part)
        return jnp.concatenate(blocks, axis=0)

    upper = CELLS - 1
    own_faces = natural([[v_dir[0, d, c : c + 1, :] for c in range(3)] for d in range(3)], upper)
    loads[4].wait()
    react0 = split(v_react[0])
    react1 = block_mean(react0, 1)
    react2 = block_mean(react1, 2)
    diag0 = broad([r + 6.0 for r in react0])
    scale0 = broad([DAMPING / (r + 6.0) for r in react0])
    scale1 = broad([DAMPING / (r + 6.0 * 0.25) for r in react1])
    scale2 = [DAMPING / (r + 6.0 * 0.0625) for r in react2]

    for copy in faces:
        copy.wait_recv()
    under = natural([[halo[d, c : c + 1, :] for c in range(3)] for d in range(3)], 0)
    source = own_faces - under
    base = join(local_solve(split(source), diag0, scale0, scale1, scale2))

    def extract(edge):
        mask_y = tile3(y_lane == edge)
        mask_z = tile3(z_lane == edge)
        in_y = collect(exact_dot(jnp.where(mask_y, base, 0.0), table[same]))
        in_z = collect(exact_dot(jnp.where(mask_z, base, 0.0), table[from_z]))
        in_x = [base[CELLS * c + edge : CELLS * c + edge + 1] for c in range(3)]
        return [in_x, in_y, in_z]

    lower_rows = extract(0)
    for d in range(3):
        for c in range(3):
            face_send[d, c : c + 1, :] = lower_rows[d][c]
    backs = [
        pltpu.make_async_remote_copy(
            src_ref=face_send.at[d],
            dst_ref=after.at[d],
            send_sem=back_send.at[d],
            recv_sem=back_recv.at[d],
            device_id=below[d],
            device_id_type=MESH,
        )
        for d in (1, 2, 0)
    ]
    for copy in backs:
        copy.start()

    all_of(gather, n_sub, sub_peer, 0).wait_recv()
    everyone = gather[...]
    packet2[...] = jnp.sum(everyone, axis=0)
    gather2[region] = packet2[...]
    send_all(packet2, gather2.at[region], n_region, region_peer, 1)
    loads[5].wait()
    rows_y = n_sub // DOM_Z
    lane_a = iota((rows_y, 128), 1)
    quads = []
    for b in range(DOM_Z):
        quads.append(jnp.concatenate([gather[DOM_Z * a + b, 0:1, :] for a in range(rows_y)], axis=0))

    def shifted(v, by):
        return pltpu.roll(v, by % 128, 1) if by % 128 else v

    packed = [
        jnp.where(lane_a < 96, quads[0], shifted(quads[1], 96)),
        jnp.where(lane_a < 64, shifted(quads[1], -32), shifted(quads[2], 64)),
        jnp.where(lane_a < 32, shifted(quads[2], -64), shifted(quads[3], 32)),
    ]
    lanes = jnp.zeros((96, 128), F32)
    for a in range(rows_y):
        for j in range(3):
            at = (3 * a + j) * 128
            lanes = lanes + v_rows[0, :, at : at + 128] * packed[j][a : a + 1, :]

    def lane_total(v):
        tall = jnp.concatenate([v, jnp.zeros((32, 128), F32)], axis=0)
        return jnp.sum(jnp.transpose(tall), axis=0, keepdims=True)

    region_row = lane_total(lanes)
    part = jnp.sum(source * base, axis=0, keepdims=True)
    part = part[:, :128] + part[:, 128:] + primal_row * region_row
    packet3[...] = jnp.broadcast_to(part, (8, 128))
    gather3[sub] = packet3[...]
    send_all(packet3, gather3.at[sub], n_sub, sub_peer, 2)

    all_of(gather2, n_region, region_peer, 1).wait_recv()
    whole = jnp.sum(gather2[...], axis=0)
    squares_all = jnp.sum(jnp.where(lane_row == 96, whole[0:1, :], 0.0))
    total = jnp.concatenate([whole[1:2, :], whole[2:3, :], whole[3:4, :]], axis=1)
    loads[6].wait()
    top = lax.dot_general(
        jnp.broadcast_to(total, (8, 384)),
        v_ginv[...],
        (((1,), (1,)), ((), ())),
        precision=lax.Precision.HIGHEST,
        preferred_element_type=F32,
    )[0:1]
    energy = jnp.sum(total * top)
    weighted = v_map[0] * top
    lanes = weighted[:, :128] + weighted[:, 128:256] + weighted[:, 256:]
    lifted = region_row + lane_total(lanes)
    key_row = jnp.broadcast_to(index_row >> 7, (32, 128))
    placed = jnp.where(key_row == iota((32, 128), 0), jnp.broadcast_to(lifted, (32, 128)), 0.0)
    placed = exact_dot(placed, hit.astype(BF16))

    def lifted_row(d, c):
        r = (d * 3 + c) * 2
        return jnp.concatenate([placed[r : r + 1], placed[r + 1 : r + 2]], axis=1)

    lifted_rows = [[lifted_row(d, c) for c in range(3)] for d in range(3)]
    field = base + natural(lifted_rows, upper)
    upper_rows = extract(upper)
    for c in range(3):
        velocity[0, c] = field[CELLS * c : CELLS * c + CELLS]

    all_of(gather3, n_sub, sub_peer, 2).wait_recv()
    packet4[...] = jnp.sum(gather3[...], axis=0)
    gather4[region] = packet4[...]
    send_all(packet4, gather4.at[region], n_region, region_peer, 3)

    for copy in backs:
        copy.wait_recv()
    loads[7].wait()
    loads[8].wait()
    v = [field[CELLS * c : CELLS * c + CELLS] for c in range(3)]
    edge_x = jnp.broadcast_to(after[0, 0:1, :], (CELLS, FACE))
    edge_y = exact_dot(spread([after[1, 1:2, :]]), table[same])
    edge_z = exact_dot(spread([after[2, 2:3, :]]), table[to_z])
    step_x = jnp.where(x_row == upper, edge_x, pltpu.roll(v[0], CELLS - 1, 0)) - v[0]
    step_y = jnp.where(y_lane == upper, edge_y, pltpu.roll(v[1], FACE - CELLS, 1)) - v[1]
    step_z = jnp.where(z_lane == upper, edge_z, pltpu.roll(v[2], FACE - 1, 1)) - v[2]
    pressure[0] = -v_visc[0] * (step_x + step_y + step_z)
    jumps = []
    for d in range(3):
        rows = [upper_rows[d][c] + lifted_rows[d][c] for c in range(3)]
        jumps.append(jnp.concatenate(rows, axis=0) - after[d])

    all_of(gather4, n_region, region_peer, 3).wait_recv()
    curvature = jnp.sum(jnp.sum(gather4[...], axis=0)[0:1]) + energy
    alpha = squares_all / curvature
    for d in range(3):
        new_multipliers[0, d] = v_mult[0, d] + alpha * v_dir[0, d]
        new_residual[0, d] = v_res[0, d] - alpha * jumps[d]

    for copy in faces:
        copy.wait_send()
    for copy in backs:
        copy.wait_send()
    all_of(gather, n_sub, sub_peer, 0).wait_send()
    all_of(gather2, n_region, region_peer, 1).wait_send()
    all_of(gather3, n_sub, sub_peer, 2).wait_send()
    all_of(gather4, n_region, region_peer, 3).wait_send()


def solution(mesh):
    n_region = mesh.shape["region"]
    n_sub = mesh.shape["sub"]

    def body(*args):
        shapes = [a.shape for a in args]
        vmem = [pltpu.VMEM(a.shape, a.dtype) for a in args[:8]] + [pltpu.VMEM(args[8].shape, F32)]
        like = (args[0], args[2])
        outs = [jax.ShapeDtypeStruct(a.shape, F32) for a in like]
        outs.append(jax.ShapeDtypeStruct((1, 3, CELLS, FACE), F32))
        outs.append(jax.ShapeDtypeStruct((1, CELLS, FACE), F32))
        return tuple(
            pl.pallas_call(
                functools.partial(kernel, n_region, n_sub),
                out_shape=outs,
                in_specs=[pl.BlockSpec(memory_space=pl.ANY)] * 9,
                out_specs=[pl.BlockSpec(memory_space=pltpu.VMEM)] * 4,
                scratch_shapes=vmem
                + [
                    pltpu.VMEM((3, FACE, FACE), BF16),
                    pltpu.VMEM((8, 128), jnp.int32),
                    pltpu.VMEM((3, 3, FACE), F32),
                    pltpu.VMEM((3, 3, FACE), F32),
                    pltpu.VMEM((3, 3, FACE), F32),
                    pltpu.VMEM((4, 128), F32),
                    pltpu.VMEM((n_sub, 4, 128), F32),
                    pltpu.VMEM((4, 128), F32),
                    pltpu.VMEM((n_region, 4, 128), F32),
                    pltpu.VMEM((8, 128), F32),
                    pltpu.VMEM((n_sub, 8, 128), F32),
                    pltpu.VMEM((8, 128), F32),
                    pltpu.VMEM((n_region, 8, 128), F32),
                    pltpu.SemaphoreType.DMA((9,)),
                    pltpu.SemaphoreType.DMA((3,)),
                    pltpu.SemaphoreType.DMA((3,)),
                    pltpu.SemaphoreType.DMA((3,)),
                    pltpu.SemaphoreType.DMA((3,)),
                    pltpu.SemaphoreType.DMA((4,)),
                    pltpu.SemaphoreType.DMA((4,)),
                ],
                compiler_params=pltpu.CompilerParams(collective_id=0, has_side_effects=True),
                name="feti",
            )(*args)
        )

    in_specs = (
        P(("region", "sub"), None, None, None),
        P(("region", "sub"), None, None, None),
        P(("region", "sub"), None, None, None),
        P(("region", "sub"), None, None),
        P(("region", "sub"), None, None),
        P(("region", "sub"), None),
        P("region", "sub", None),
        P(("region", "sub"), None, None),
        P(),
    )
    out_specs = (
        P(("region", "sub"), None, None, None),
        P(("region", "sub"), None, None, None),
        P(("region", "sub"), None, None, None),
        P(("region", "sub"), None, None),
    )
    return jax.shard_map(body, mesh=mesh, in_specs=in_specs, out_specs=out_specs, check_vma=False)
```

```python
import functools

import jax
import jax.numpy as jnp
from jax import lax
from jax.experimental import pallas as pl
from jax.experimental.pallas import tpu as pltpu
from jax.sharding import PartitionSpec as P

DOM_Z = 4
COARSE_SWEEPS = 8
CELLS = 16
FACE = 256
DAMPING = 0.8
VMEM_LIMIT = 16 * 1024 * 1024
KEEP = 0.2
MESH = pl.DeviceIdType.MESH
F32 = jnp.float32
BF16 = jnp.bfloat16


def iota(shape, axis):
    return lax.broadcasted_iota(jnp.int32, shape, axis)


def split(field):
    lead = field.shape[0] // CELLS
    cubic = field.reshape(lead, CELLS, FACE)
    return [cubic[:, 8 * i : 8 * i + 8, 128 * j : 128 * j + 128] for i in (0, 1) for j in (0, 1)]


def join(parts):
    low = jnp.concatenate([parts[0], parts[1]], axis=2)
    high = jnp.concatenate([parts[2], parts[3]], axis=2)
    whole = jnp.concatenate([low, high], axis=1)
    return whole.reshape(whole.shape[0] * CELLS, FACE)


def neighbours(parts, step):
    shape = parts[0].shape
    x = iota(shape, 1)
    lane = iota(shape, 2)
    y = lane >> 4
    z = lane & 15

    def roll(v, by, axis):
        return pltpu.roll(v, by % v.shape[axis], axis)

    sums = []
    ys_up = [roll(v, 16 * step, 2) for v in parts]
    ys_down = ys_up if step == 4 else [roll(v, -16 * step, 2) for v in parts]
    xs_up = [roll(v, step, 1) for v in parts]
    xs_down = xs_up if step == 4 else [roll(v, -step, 1) for v in parts]
    for i in (0, 1):
        for j in (0, 1):
            k = 2 * i + j
            v = parts[k]
            total = jnp.where(z >= step, roll(v, step, 2), 0.0)
            total = total + jnp.where(z < CELLS - step, roll(v, -step, 2), 0.0)
            before = ys_up[k - 1] if j == 1 else 0.0
            total = total + jnp.where(y >= step, ys_up[k], before)
            after = ys_down[k + 1] if j == 0 else 0.0
            total = total + jnp.where(y < 8 - step, ys_down[k], after)
            before = xs_up[k - 2] if i == 1 else 0.0
            total = total + jnp.where(x >= step, xs_up[k], before)
            after = xs_down[k + 2] if i == 0 else 0.0
            total = total + jnp.where(x < 8 - step, xs_down[k], after)
            sums.append(total)
    return sums


def block_mean(parts, step):
    shape = parts[0].shape
    x = iota(shape, 1)
    lane = iota(shape, 2)

    def pair(v, by, axis, even):
        count = v.shape[axis]
        return v + jnp.where(even, pltpu.roll(v, count - by, axis), pltpu.roll(v, by, axis))

    result = []
    for v in parts:
        v = pair(v, step, 2, (lane & step) == 0)
        v = pair(v, 16 * step, 2, ((lane >> 4) & step) == 0)
        v = pair(v, step, 1, (x & step) == 0)
        result.append(v * 0.125)
    return result


def merge(parts):
    spot = iota(parts[0].shape[1:], 1) & 3
    return [jnp.where(spot == 0, v[0], jnp.where(spot == 1, v[1], v[2]))[None] for v in parts]


def unmerge(parts):
    result = []
    for v in parts:
        v = v[0]
        spot = iota(v.shape, 1) & 3
        moved = {by: pltpu.roll(v, by % 128, 1) if by else v for by in range(-2, 4)}
        comps = []
        for c in range(3):
            value = moved[3 - c]
            for t in (2, 1, 0):
                value = jnp.where(spot == t, moved[t - c], value)
            comps.append(value)
        result.append(jnp.stack(comps, axis=0))
    return result


def broad(parts):
    return [jnp.broadcast_to(v, (3,) + v.shape[1:]) for v in parts]


def coarse_solve(source, scale2):
    b = merge(source)
    wb = [w * s for w, s in zip(scale2, b)]
    v = wb
    for _ in range(COARSE_SWEEPS - 1):
        near = neighbours(v, 4)
        v = [KEEP * a + (c + (w * 0.0625) * n) for a, c, w, n in zip(v, wb, scale2, near)]
    return unmerge(v)


def middle_solve(source, scale1, scale2):
    wb = [w * s for w, s in zip(scale1, source)]
    near = neighbours(wb, 2)
    remain = [KEEP * s + 0.25 * n for s, n in zip(source, near)]
    coarse = coarse_solve(block_mean(remain, 2), scale2)
    v = [a + c for a, c in zip(wb, coarse)]
    near = neighbours(v, 2)
    return [KEEP * a + (c + (w * 0.25) * n) for a, c, w, n in zip(v, wb, scale1, near)]


def local_solve(source, diag0, scale0, scale1, scale2):
    wb = [w * s for w, s in zip(scale0, source)]
    v = None
    for cycle in range(2):
        if cycle == 0:
            v = wb
            remain = [KEEP * s + n for s, n in zip(source, neighbours(v, 1))]
        else:
            near = neighbours(v, 1)
            v = [KEEP * a + (c + w * n) for a, c, w, n in zip(v, wb, scale0, near)]
            near = neighbours(v, 1)
            remain = [(s - d * a) + n for s, d, a, n in zip(source, diag0, v, near)]
        coarse = middle_solve(block_mean(remain, 1), scale1, scale2)
        v = [a + c for a, c in zip(v, coarse)]
        near = neighbours(v, 1)
        v = [KEEP * a + (c + w * n) for a, c, w, n in zip(v, wb, scale0, near)]
    return v


def exact_dot(left, right):
    high = left.astype(BF16)
    rest = left - high.astype(F32)
    mid = rest.astype(BF16)
    low = (rest - mid.astype(F32)).astype(BF16)
    dot = functools.partial(jnp.dot, preferred_element_type=F32)
    return dot(high, right) + (dot(mid, right) + dot(low, right))


def spread(rows):
    own = (iota((CELLS, FACE), 1) >> 4) == iota((CELLS, FACE), 0)
    return jnp.concatenate([jnp.where(own, jnp.broadcast_to(r, (CELLS, FACE)), 0.0) for r in rows], axis=0)


def collect(field):
    own = (iota((CELLS, FACE), 1) >> 4) == iota((CELLS, FACE), 0)
    return [
        jnp.sum(jnp.where(own, field[CELLS * c : CELLS * c + CELLS], 0.0), axis=0, keepdims=True)
        for c in range(3)
    ]


def kernel(
    n_region,
    n_sub,
    direction,
    residual,
    reaction,
    viscosity,
    primal_index,
    region_inverse,
    coarse_map,
    global_inverse,
    jump,
    alpha,
    velocity,
    pressure,
    v_dir,
    v_res,
    v_react,
    v_visc,
    v_index,
    v_rows,
    v_map,
    v_ginv,
    table,
    padded_index,
    halo,
    face_send,
    after,
    packet,
    gather,
    packet2,
    gather2,
    packet3,
    gather3,
    packet4,
    gather4,
    load_sem,
    halo_send,
    halo_recv,
    back_send,
    back_recv,
    sum_send,
    sum_recv,
):
    region = lax.axis_index("region")
    sub = lax.axis_index("sub")

    def sub_peer(i):
        return (region, lax.rem(sub + i, n_sub))

    def region_peer(i):
        return (lax.rem(region + i, n_region), sub)

    loads = [
        pltpu.make_async_copy(src, dst, load_sem.at[i])
        for i, (src, dst) in enumerate(
            (
                (direction, v_dir),
                (primal_index, v_index),
                (coarse_map, v_map),
                (residual, v_res),
                (reaction, v_react),
                (region_inverse, v_rows),
                (global_inverse, v_ginv),
                (viscosity, v_visc),
            )
        )
    ]
    for load in loads:
        load.start()

    barrier = pltpu.get_barrier_semaphore()

    def greet_sub(i, carry):
        pl.semaphore_signal(barrier, inc=1, device_id=sub_peer(i), device_id_type=MESH)
        return carry

    def greet_region(i, carry):
        pl.semaphore_signal(barrier, inc=1, device_id=region_peer(i), device_id_type=MESH)
        return carry

    lax.fori_loop(1, n_sub, greet_sub, 0)
    lax.fori_loop(1, n_region, greet_region, 0)

    def send_all(src, dst_of_me, count, peer, index):
        def one(i, carry):
            pltpu.make_async_remote_copy(
                src_ref=src,
                dst_ref=dst_of_me,
                send_sem=sum_send.at[index],
                recv_sem=sum_recv.at[index],
                device_id=peer(i),
                device_id_type=MESH,
            ).start()
            return carry

        lax.fori_loop(1, count, one, 0)

    def all_of(buffer, count, peer, index):
        part = buffer.at[pl.ds(0, count - 1)]
        return pltpu.make_async_remote_copy(
            src_ref=part,
            dst_ref=part,
            send_sem=sum_send.at[index],
            recv_sem=sum_recv.at[index],
            device_id=peer(1),
            device_id_type=MESH,
        )

    row_i = iota((FACE, FACE), 0)
    col_i = iota((FACE, FACE), 1)
    table[0] = jnp.where((row_i & 15) == (col_i & 15), 1.0, 0.0).astype(BF16)
    table[1] = jnp.where((row_i & 15) == (col_i >> 4), 1.0, 0.0).astype(BF16)
    table[2] = jnp.where((row_i >> 4) == (col_i & 15), 1.0, 0.0).astype(BF16)

    loads[0].wait()
    loads[1].wait()
    padded_index[...] = jnp.full((8, 128), -1, jnp.int32)
    padded_index[0:1, 0:96] = v_index[...]
    index_row = padded_index[0:1, :]
    index_col = jnp.transpose(jnp.broadcast_to(index_row.astype(F32), (128, 128))).astype(jnp.int32)
    lane128 = iota((128, 128), 1)
    hit = jnp.where((index_col & 127) == lane128, 1.0, 0.0)
    key_col = index_col >> 7
    picked = jnp.zeros((128, 128), F32)
    for d in range(3):
        for c in range(3):
            for h in range(2):
                r = (d * 3 + c) * 2 + h
                values = v_dir[d, c, :, 128 * h : 128 * h + 128]
                picked = jnp.where(key_col == r, jnp.broadcast_to(values, (128, 128)), picked)
    picked = picked * hit
    primal_row = jnp.sum(jnp.transpose(picked), axis=0, keepdims=True)
    primal_col = jnp.sum(picked, axis=1, keepdims=True)[:96]
    loads[2].wait()
    share = jnp.sum(primal_col * v_map[0], axis=0, keepdims=True)
    loads[3].wait()
    squares = jnp.sum(v_res[...] * v_res[...])
    lane_row = iota((1, 128), 1)
    packet[0:1, :] = jnp.where(lane_row < 96, primal_row, squares)
    for j in range(3):
        packet[j + 1 : j + 2, :] = share[:, 128 * j : 128 * j + 128]
    gather[sub] = packet[...]

    pl.semaphore_wait(barrier, n_sub - 1 + n_region - 1)

    above = (region_peer(1), sub_peer(DOM_Z), sub_peer(1))
    below = (region_peer(n_region - 1), sub_peer(n_sub - DOM_Z), sub_peer(n_sub - 1))
    faces = [
        pltpu.make_async_remote_copy(
            src_ref=v_dir.at[d],
            dst_ref=halo.at[d],
            send_sem=halo_send.at[d],
            recv_sem=halo_recv.at[d],
            device_id=above[d],
            device_id_type=MESH,
        )
        for d in (1, 2, 0)
    ]
    for copy in faces:
        copy.start()
    send_all(packet, gather.at[sub], n_sub, sub_peer, 0)

    lane = iota((CELLS, FACE), 1)
    y_lane = lane >> 4
    z_lane = lane & 15
    x_row = iota((CELLS, FACE), 0)
    same, to_z, from_z = 0, 1, 2

    def tile3(mask):
        return jnp.concatenate([mask] * 3, axis=0)

    def natural(face_rows, edge):
        in_y = exact_dot(spread(face_rows[1]), table[same])
        in_z = exact_dot(spread(face_rows[2]), table[to_z])
        blocks = []
        for c in range(3):
            part = jnp.where(x_row == edge, jnp.broadcast_to(face_rows[0][c], (CELLS, FACE)), 0.0)
            part = part + jnp.where(y_lane == edge, in_y[CELLS * c : CELLS * c + CELLS], 0.0)
            part = part + jnp.where(z_lane == edge, in_z[CELLS * c : CELLS * c + CELLS], 0.0)
            blocks.append(part)
        return jnp.concatenate(blocks, axis=0)

    upper = CELLS - 1
    own_faces = natural([[v_dir[d, c] for c in range(3)] for d in range(3)], upper)
    loads[4].wait()
    react0 = split(v_react[0])
    react1 = block_mean(react0, 1)
    react2 = block_mean(react1, 2)
    diag0 = broad([r + 6.0 for r in react0])
    scale0 = broad([DAMPING / (r + 6.0) for r in react0])
    scale1 = broad([DAMPING / (r + 6.0 * 0.25) for r in react1])
    scale2 = [DAMPING / (r + 6.0 * 0.0625) for r in react2]

    for copy in faces:
        copy.wait_recv()
    under = natural([[halo[d, c] for c in range(3)] for d in range(3)], 0)
    source = own_faces - under
    base = join(local_solve(split(source), diag0, scale0, scale1, scale2))

    def extract(edge):
        mask_y = tile3(y_lane == edge)
        mask_z = tile3(z_lane == edge)
        in_y = collect(exact_dot(jnp.where(mask_y, base, 0.0), table[same]))
        in_z = collect(exact_dot(jnp.where(mask_z, base, 0.0), table[from_z]))
        in_x = [base[CELLS * c + edge : CELLS * c + edge + 1] for c in range(3)]
        return [in_x, in_y, in_z]

    lower_rows = extract(0)
    for d in range(3):
        for c in range(3):
            face_send[d, c] = lower_rows[d][c]
    backs = [
        pltpu.make_async_remote_copy(
            src_ref=face_send.at[d],
            dst_ref=after.at[d],
            send_sem=back_send.at[d],
            recv_sem=back_recv.at[d],
            device_id=below[d],
            device_id_type=MESH,
        )
        for d in (1, 2, 0)
    ]
    for copy in backs:
        copy.start()

    all_of(gather, n_sub, sub_peer, 0).wait_recv()
    everyone = gather[...]
    packet2[...] = jnp.sum(everyone, axis=0)
    gather2[region] = packet2[...]
    send_all(packet2, gather2.at[region], n_region, region_peer, 1)
    loads[5].wait()
    rows_y = n_sub // DOM_Z
    lane_a = iota((rows_y, 128), 1)
    quads = []
    for b in range(DOM_Z):
        quads.append(jnp.concatenate([gather[DOM_Z * a + b, 0:1, :] for a in range(rows_y)], axis=0))

    def shifted(v, by):
        return pltpu.roll(v, by % 128, 1) if by % 128 else v

    packed = [
        jnp.where(lane_a < 96, quads[0], shifted(quads[1], 96)),
        jnp.where(lane_a < 64, shifted(quads[1], -32), shifted(quads[2], 64)),
        jnp.where(lane_a < 32, shifted(quads[2], -64), shifted(quads[3], 32)),
    ]
    lanes = jnp.zeros((96, 128), F32)
    for a in range(rows_y):
        for j in range(3):
            at = (3 * a + j) * 128
            lanes = lanes + v_rows[0, :, at : at + 128] * packed[j][a : a + 1, :]

    def lane_total(v):
        tall = jnp.concatenate([v, jnp.zeros((32, 128), F32)], axis=0)
        return jnp.sum(jnp.transpose(tall), axis=0, keepdims=True)

    region_row = lane_total(lanes)
    part = jnp.sum(source * base, axis=0, keepdims=True)
    part = part[:, :128] + part[:, 128:] + primal_row * region_row
    packet3[...] = jnp.broadcast_to(part, (8, 128))
    gather3[sub] = packet3[...]
    send_all(packet3, gather3.at[sub], n_sub, sub_peer, 2)

    all_of(gather2, n_region, region_peer, 1).wait_recv()
    whole = jnp.sum(gather2[...], axis=0)
    squares_all = jnp.sum(jnp.where(lane_row == 96, whole[0:1, :], 0.0))
    total = jnp.concatenate([whole[1:2, :], whole[2:3, :], whole[3:4, :]], axis=1)
    loads[6].wait()
    top = lax.dot_general(
        jnp.broadcast_to(total, (8, 384)),
        v_ginv[...],
        (((1,), (1,)), ((), ())),
        precision=lax.Precision.HIGHEST,
        preferred_element_type=F32,
    )[0:1]
    energy = jnp.sum(total * top)
    weighted = v_map[0] * top
    lanes = weighted[:, :128] + weighted[:, 128:256] + weighted[:, 256:]
    lifted = region_row + lane_total(lanes)
    key_row = jnp.broadcast_to(index_row >> 7, (32, 128))
    placed = jnp.where(key_row == iota((32, 128), 0), jnp.broadcast_to(lifted, (32, 128)), 0.0)
    placed = exact_dot(placed, hit.astype(BF16))

    def lifted_row(d, c):
        r = (d * 3 + c) * 2
        return jnp.concatenate([placed[r : r + 1], placed[r + 1 : r + 2]], axis=1)

    lifted_rows = [[lifted_row(d, c) for c in range(3)] for d in range(3)]
    field = base + natural(lifted_rows, upper)
    upper_rows = extract(upper)
    for c in range(3):
        velocity[0, c] = field[CELLS * c : CELLS * c + CELLS]

    all_of(gather3, n_sub, sub_peer, 2).wait_recv()
    packet4[...] = jnp.sum(gather3[...], axis=0)
    gather4[region] = packet4[...]
    send_all(packet4, gather4.at[region], n_region, region_peer, 3)

    for copy in backs:
        copy.wait_recv()
    loads[7].wait()
    v = [field[CELLS * c : CELLS * c + CELLS] for c in range(3)]
    edge_x = jnp.broadcast_to(after[0, 0], (CELLS, FACE))
    edge_y = exact_dot(spread([after[1, 1]]), table[same])
    edge_z = exact_dot(spread([after[2, 2]]), table[to_z])
    step_x = jnp.where(x_row == upper, edge_x, pltpu.roll(v[0], CELLS - 1, 0)) - v[0]
    step_y = jnp.where(y_lane == upper, edge_y, pltpu.roll(v[1], FACE - CELLS, 1)) - v[1]
    step_z = jnp.where(z_lane == upper, edge_z, pltpu.roll(v[2], FACE - 1, 1)) - v[2]
    pressure[0] = -v_visc[0] * (step_x + step_y + step_z)
    for d in range(3):
        for c in range(3):
            jump[d, c] = upper_rows[d][c] + lifted_rows[d][c] - after[d, c]

    all_of(gather4, n_region, region_peer, 3).wait_recv()
    curvature = jnp.sum(jnp.sum(gather4[...], axis=0)[0:1]) + energy
    alpha[...] = jnp.broadcast_to(squares_all / curvature, (8, 128))

    for copy in faces:
        copy.wait_send()
    for copy in backs:
        copy.wait_send()
    all_of(gather, n_sub, sub_peer, 0).wait_send()
    all_of(gather2, n_region, region_peer, 1).wait_send()
    all_of(gather3, n_sub, sub_peer, 2).wait_send()
    all_of(gather4, n_region, region_peer, 3).wait_send()


def finish(multipliers, direction, residual, jump, alpha, velocity, pressure, *outs):
    step = jnp.broadcast_to(alpha[0:1, 0:1], (1, FACE))
    for d in range(3):
        for c in range(3):
            outs[0][d, c] = multipliers[d, c] + step * direction[d, c]
            outs[1][d, c] = residual[d, c] - step * jump[d, c]
    outs[2][...] = velocity[...]
    outs[3][...] = pressure[...]


def solution(mesh):
    n_region = mesh.shape["region"]
    n_sub = mesh.shape["sub"]

    def body(multipliers, direction, residual, *rest):
        faces = [a.reshape(3, 3, 1, FACE) for a in (multipliers, direction, residual)]
        args = [pltpu.with_memory_space_constraint(a, pltpu.HBM) for a in (faces[1], faces[2]) + rest]
        face = jax.ShapeDtypeStruct((3, 3, 1, FACE), F32)
        cells = jax.ShapeDtypeStruct((1, 3, CELLS, FACE), F32)
        scalar_cells = jax.ShapeDtypeStruct((1, CELLS, FACE), F32)
        inner = pl.pallas_call(
            functools.partial(kernel, n_region, n_sub),
            out_shape=[face, jax.ShapeDtypeStruct((8, 128), F32), cells, scalar_cells],
            in_specs=[pl.BlockSpec(memory_space=pltpu.HBM)] * 8,
            out_specs=[pl.BlockSpec(memory_space=pltpu.VMEM)] * 4,
            scratch_shapes=[pltpu.VMEM(a.shape, a.dtype) for a in args]
            + [
                pltpu.VMEM((3, FACE, FACE), BF16),
                pltpu.VMEM((8, 128), jnp.int32),
                pltpu.VMEM((3, 3, 1, FACE), F32),
                pltpu.VMEM((3, 3, 1, FACE), F32),
                pltpu.VMEM((3, 3, 1, FACE), F32),
                pltpu.VMEM((4, 128), F32),
                pltpu.VMEM((n_sub, 4, 128), F32),
                pltpu.VMEM((4, 128), F32),
                pltpu.VMEM((n_region, 4, 128), F32),
                pltpu.VMEM((8, 128), F32),
                pltpu.VMEM((n_sub, 8, 128), F32),
                pltpu.VMEM((8, 128), F32),
                pltpu.VMEM((n_region, 8, 128), F32),
                pltpu.SemaphoreType.DMA((8,)),
                pltpu.SemaphoreType.DMA((3,)),
                pltpu.SemaphoreType.DMA((3,)),
                pltpu.SemaphoreType.DMA((3,)),
                pltpu.SemaphoreType.DMA((3,)),
                pltpu.SemaphoreType.DMA((4,)),
                pltpu.SemaphoreType.DMA((4,)),
            ],
            compiler_params=pltpu.CompilerParams(
                collective_id=0, has_side_effects=True, vmem_limit_bytes=VMEM_LIMIT
            ),
            name="feti",
        )
        jump, alpha, velocity, pressure = inner(*args)
        outs = pl.pallas_call(
            finish,
            out_shape=[face, face, cells, scalar_cells],
            in_specs=[pl.BlockSpec(memory_space=pltpu.VMEM)] * 7,
            out_specs=[pl.BlockSpec(memory_space=pltpu.VMEM)] * 4,
            compiler_params=pltpu.CompilerParams(vmem_limit_bytes=VMEM_LIMIT),
            name="finish",
        )(*faces, jump, alpha, velocity, pressure)
        shape = multipliers.shape
        return outs[0].reshape(shape), outs[1].reshape(shape), outs[2], outs[3]

    in_specs = (
        P(("region", "sub"), None, None, None),
        P(("region", "sub"), None, None, None),
        P(("region", "sub"), None, None, None),
        P(("region", "sub"), None, None),
        P(("region", "sub"), None, None),
        P(("region", "sub"), None),
        P("region", "sub", None),
        P(("region", "sub"), None, None),
        P(),
    )
    out_specs = (
        P(("region", "sub"), None, None, None),
        P(("region", "sub"), None, None, None),
        P(("region", "sub"), None, None, None),
        P(("region", "sub"), None, None),
    )
    return jax.shard_map(body, mesh=mesh, in_specs=in_specs, out_specs=out_specs, check_vma=False)
```

```python
import functools

import jax
import jax.numpy as jnp
from jax import lax
from jax.experimental import pallas as pl
from jax.experimental.pallas import tpu as pltpu
from jax.sharding import PartitionSpec as P

DOM_Z = 4
Z_LINE = 8
COARSE_SWEEPS = 8
CELLS = 16
FACE = 256
DAMPING = 0.8
VMEM_LIMIT = 16 * 1024 * 1024
KEEP = 0.2
MESH = pl.DeviceIdType.MESH
F32 = jnp.float32
BF16 = jnp.bfloat16


def iota(shape, axis):
    return lax.broadcasted_iota(jnp.int32, shape, axis)


def split(field):
    lead = field.shape[0] // CELLS
    cubic = field.reshape(lead, CELLS, FACE)
    return [cubic[:, 8 * i : 8 * i + 8, 128 * j : 128 * j + 128] for i in (0, 1) for j in (0, 1)]


def join(parts):
    low = jnp.concatenate([parts[0], parts[1]], axis=2)
    high = jnp.concatenate([parts[2], parts[3]], axis=2)
    whole = jnp.concatenate([low, high], axis=1)
    return whole.reshape(whole.shape[0] * CELLS, FACE)


def neighbours(parts, step):
    shape = parts[0].shape
    x = iota(shape, 1)
    lane = iota(shape, 2)
    y = lane >> 4
    z = lane & 15

    def roll(v, by, axis):
        return pltpu.roll(v, by % v.shape[axis], axis)

    sums = []
    ys_up = [roll(v, 16 * step, 2) for v in parts]
    ys_down = ys_up if step == 4 else [roll(v, -16 * step, 2) for v in parts]
    xs_up = [roll(v, step, 1) for v in parts]
    xs_down = xs_up if step == 4 else [roll(v, -step, 1) for v in parts]
    for i in (0, 1):
        for j in (0, 1):
            k = 2 * i + j
            v = parts[k]
            total = jnp.where(z >= step, roll(v, step, 2), 0.0)
            total = total + jnp.where(z < CELLS - step, roll(v, -step, 2), 0.0)
            before = ys_up[k - 1] if j == 1 else 0.0
            total = total + jnp.where(y >= step, ys_up[k], before)
            after = ys_down[k + 1] if j == 0 else 0.0
            total = total + jnp.where(y < 8 - step, ys_down[k], after)
            before = xs_up[k - 2] if i == 1 else 0.0
            total = total + jnp.where(x >= step, xs_up[k], before)
            after = xs_down[k + 2] if i == 0 else 0.0
            total = total + jnp.where(x < 8 - step, xs_down[k], after)
            sums.append(total)
    return sums


def block_mean(parts, step):
    shape = parts[0].shape
    x = iota(shape, 1)
    lane = iota(shape, 2)

    def pair(v, by, axis, even):
        count = v.shape[axis]
        return v + jnp.where(even, pltpu.roll(v, count - by, axis), pltpu.roll(v, by, axis))

    result = []
    for v in parts:
        v = pair(v, step, 2, (lane & step) == 0)
        v = pair(v, 16 * step, 2, ((lane >> 4) & step) == 0)
        v = pair(v, step, 1, (x & step) == 0)
        result.append(v * 0.125)
    return result


def merge(parts):
    spot = iota(parts[0].shape[1:], 1) & 3
    return [jnp.where(spot == 0, v[0], jnp.where(spot == 1, v[1], v[2]))[None] for v in parts]


def unmerge(parts):
    result = []
    for v in parts:
        v = v[0]
        spot = iota(v.shape, 1) & 3
        moved = {by: pltpu.roll(v, by % 128, 1) if by else v for by in range(-2, 4)}
        comps = []
        for c in range(3):
            value = moved[3 - c]
            for t in (2, 1, 0):
                value = jnp.where(spot == t, moved[t - c], value)
            comps.append(value)
        result.append(jnp.stack(comps, axis=0))
    return result


def broad(parts):
    return [jnp.broadcast_to(v, (3,) + v.shape[1:]) for v in parts]


def coarse_solve(source, scale2):
    b = merge(source)
    wb = [w * s for w, s in zip(scale2, b)]
    v = wb
    for _ in range(COARSE_SWEEPS - 1):
        near = neighbours(v, 4)
        v = [KEEP * a + (c + (w * 0.0625) * n) for a, c, w, n in zip(v, wb, scale2, near)]
    return unmerge(v)


def middle_solve(source, scale1, scale2):
    wb = [w * s for w, s in zip(scale1, source)]
    near = neighbours(wb, 2)
    remain = [KEEP * s + 0.25 * n for s, n in zip(source, near)]
    coarse = coarse_solve(block_mean(remain, 2), scale2)
    v = [a + c for a, c in zip(wb, coarse)]
    near = neighbours(v, 2)
    return [KEEP * a + (c + (w * 0.25) * n) for a, c, w, n in zip(v, wb, scale1, near)]


def local_solve(source, diag0, scale0, scale1, scale2):
    wb = [w * s for w, s in zip(scale0, source)]
    v = None
    for cycle in range(2):
        if cycle == 0:
            v = wb
            remain = [KEEP * s + n for s, n in zip(source, neighbours(v, 1))]
        else:
            near = neighbours(v, 1)
            v = [KEEP * a + (c + w * n) for a, c, w, n in zip(v, wb, scale0, near)]
            near = neighbours(v, 1)
            remain = [(s - d * a) + n for s, d, a, n in zip(source, diag0, v, near)]
        coarse = middle_solve(block_mean(remain, 1), scale1, scale2)
        v = [a + c for a, c in zip(v, coarse)]
        near = neighbours(v, 1)
        v = [KEEP * a + (c + w * n) for a, c, w, n in zip(v, wb, scale0, near)]
    return v


def exact_dot(left, right):
    high = left.astype(BF16)
    rest = left - high.astype(F32)
    mid = rest.astype(BF16)
    low = (rest - mid.astype(F32)).astype(BF16)
    dot = functools.partial(jnp.dot, preferred_element_type=F32)
    return dot(high, right) + (dot(mid, right) + dot(low, right))


def spread(rows):
    own = (iota((CELLS, FACE), 1) >> 4) == iota((CELLS, FACE), 0)
    return jnp.concatenate([jnp.where(own, jnp.broadcast_to(r, (CELLS, FACE)), 0.0) for r in rows], axis=0)


def collect(field):
    own = (iota((CELLS, FACE), 1) >> 4) == iota((CELLS, FACE), 0)
    return [
        jnp.sum(jnp.where(own, field[CELLS * c : CELLS * c + CELLS], 0.0), axis=0, keepdims=True)
        for c in range(3)
    ]


def kernel(
    n_region,
    n_sub,
    direction,
    residual,
    reaction,
    viscosity,
    primal_index,
    region_inverse,
    coarse_map,
    global_inverse,
    jump,
    alpha,
    velocity,
    pressure,
    v_dir,
    v_res,
    v_react,
    v_visc,
    v_index,
    v_rows,
    v_map,
    v_ginv,
    table,
    padded_index,
    halo,
    face_send,
    after,
    packet,
    gather_y,
    block,
    gather,
    packet2,
    gather2,
    packet3,
    gather3,
    load_sem,
    halo_send,
    halo_recv,
    back_send,
    back_recv,
    sum_send,
    sum_recv,
):
    region = lax.axis_index("region")
    sub = lax.axis_index("sub")

    n_y = n_sub // Z_LINE
    at_y = sub // Z_LINE
    at_z = lax.rem(sub, Z_LINE)

    def sub_peer(i):
        return (region, lax.rem(sub + i, n_sub))

    def region_peer(i):
        return (lax.rem(region + i, n_region), sub)

    def y_peer(i):
        return (region, lax.rem(at_y + i, n_y) * Z_LINE + at_z)

    def z_peer(i):
        return (region, at_y * Z_LINE + lax.rem(at_z + i, Z_LINE))

    loads = [
        pltpu.make_async_copy(src, dst, load_sem.at[i])
        for i, (src, dst) in enumerate(
            (
                (direction, v_dir),
                (primal_index, v_index),
                (coarse_map, v_map),
                (residual, v_res),
                (reaction, v_react),
                (region_inverse, v_rows),
                (global_inverse, v_ginv),
                (viscosity, v_visc),
            )
        )
    ]
    for load in loads:
        load.start()

    barrier = pltpu.get_barrier_semaphore()

    near = [sub_peer(n_sub - DOM_Z), sub_peer(n_sub - 1), sub_peer(DOM_Z), sub_peer(1)]
    near += [z_peer(i) for i in range(1, Z_LINE)]
    near += [y_peer(i) for i in range(1, n_y)] + [region_peer(i) for i in range(1, n_region)]
    for peer in near:
        pl.semaphore_signal(barrier, inc=1, device_id=peer, device_id_type=MESH)

    def send_all(src, dst_of_me, peers, index):
        for peer in peers:
            pltpu.make_async_remote_copy(
                src_ref=src,
                dst_ref=dst_of_me,
                send_sem=sum_send.at[index],
                recv_sem=sum_recv.at[index],
                device_id=peer,
                device_id_type=MESH,
            ).start()

    def all_of(buffer, peers, index):
        part = buffer.at[pl.ds(0, len(peers))]
        return pltpu.make_async_remote_copy(
            src_ref=part,
            dst_ref=part,
            send_sem=sum_send.at[index],
            recv_sem=sum_recv.at[index],
            device_id=peers[0],
            device_id_type=MESH,
        )

    on_y = [y_peer(i) for i in range(1, n_y)]
    on_z = [z_peer(i) for i in range(1, Z_LINE)]
    on_region = [region_peer(i) for i in range(1, n_region)]

    at_x = region // 2
    at_c = lax.rem(region, 2)
    n_x = n_region // 2
    found = []
    for dx in range(n_x):
        for dc in range(2):
            for dy in range(n_y):
                for dz in range(Z_LINE):
                    if dx or dc or dy or dz:
                        hops = min(dx, n_x - dx) + min(dy, n_y - dy) + min(dz, Z_LINE - dz)
                        found.append((-hops, dx, dc, dy, dz))
    found.sort()
    xs = [lax.rem(at_x + i, n_x) * 2 for i in range(n_x)]
    cs = [lax.rem(at_c + i, 2) for i in range(2)]
    ys = [lax.rem(at_y + i, n_y) * Z_LINE for i in range(n_y)]
    zs = [lax.rem(at_z + i, Z_LINE) for i in range(Z_LINE)]
    everyone = [(xs[dx] + cs[dc], ys[dy] + zs[dz]) for _, dx, dc, dy, dz in found]

    row_i = iota((FACE, FACE), 0)
    col_i = iota((FACE, FACE), 1)
    table[0] = jnp.where((row_i & 15) == (col_i & 15), 1.0, 0.0).astype(BF16)
    table[1] = jnp.where((row_i & 15) == (col_i >> 4), 1.0, 0.0).astype(BF16)
    table[2] = jnp.where((row_i >> 4) == (col_i & 15), 1.0, 0.0).astype(BF16)

    loads[0].wait()
    pl.semaphore_wait(barrier, len(near))

    def face_copy(src, dst, send, recv, peer):
        return pltpu.make_async_remote_copy(
            src_ref=src, dst_ref=dst, send_sem=send, recv_sem=recv, device_id=peer, device_id_type=MESH
        )

    below = (region_peer(n_region - 1), sub_peer(n_sub - DOM_Z), sub_peer(n_sub - 1))
    faces = [
        face_copy(v_dir.at[1], halo.at[1], halo_send.at[1], halo_recv.at[1], sub_peer(DOM_Z)),
        face_copy(v_dir.at[2], halo.at[2], halo_send.at[2], halo_recv.at[2], sub_peer(1)),
        face_copy(v_dir.at[0], halo.at[0], halo_send.at[0], halo_recv.at[0], region_peer(1)),
    ]
    for copy in faces:
        copy.start()
    loads[1].wait()
    padded_index[...] = jnp.full((8, 128), -1, jnp.int32)
    padded_index[0:1, 0:96] = v_index[...]
    index_row = padded_index[0:1, :]
    index_col = jnp.transpose(jnp.broadcast_to(index_row.astype(F32), (128, 128))).astype(jnp.int32)
    lane128 = iota((128, 128), 1)
    hit = jnp.where((index_col & 127) == lane128, 1.0, 0.0)
    key_col = index_col >> 7
    picked = jnp.zeros((128, 128), F32)
    for d in range(3):
        for c in range(3):
            for h in range(2):
                r = (d * 3 + c) * 2 + h
                values = v_dir[d, c, :, 128 * h : 128 * h + 128]
                picked = jnp.where(key_col == r, jnp.broadcast_to(values, (128, 128)), picked)
    picked = picked * hit
    primal_row = jnp.sum(jnp.transpose(picked), axis=0, keepdims=True)
    primal_col = jnp.sum(picked, axis=1, keepdims=True)[:96]
    loads[2].wait()
    share = jnp.sum(primal_col * v_map[0], axis=0, keepdims=True)
    loads[3].wait()
    squares = jnp.sum(v_res[...] * v_res[...])
    lane_row = iota((1, 128), 1)
    packet[0:1, :] = jnp.where(lane_row < 96, primal_row, squares)
    for j in range(3):
        packet[j + 1 : j + 2, :] = share[:, 128 * j : 128 * j + 128]
    gather_y[at_y] = packet[...]

    send_all(packet, gather_y.at[at_y], on_y, 0)
    lane = iota((CELLS, FACE), 1)
    y_lane = lane >> 4
    z_lane = lane & 15
    x_row = iota((CELLS, FACE), 0)
    same, to_z, from_z = 0, 1, 2

    def tile3(mask):
        return jnp.concatenate([mask] * 3, axis=0)

    def natural(face_rows, edge):
        in_y = exact_dot(spread(face_rows[1]), table[same])
        in_z = exact_dot(spread(face_rows[2]), table[to_z])
        blocks = []
        for c in range(3):
            part = jnp.where(x_row == edge, jnp.broadcast_to(face_rows[0][c], (CELLS, FACE)), 0.0)
            part = part + jnp.where(y_lane == edge, in_y[CELLS * c : CELLS * c + CELLS], 0.0)
            part = part + jnp.where(z_lane == edge, in_z[CELLS * c : CELLS * c + CELLS], 0.0)
            blocks.append(part)
        return jnp.concatenate(blocks, axis=0)

    upper = CELLS - 1
    own_faces = natural([[v_dir[d, c] for c in range(3)] for d in range(3)], upper)
    loads[4].wait()
    react0 = split(v_react[0])
    react1 = block_mean(react0, 1)
    react2 = block_mean(react1, 2)
    diag0 = broad([r + 6.0 for r in react0])
    scale0 = broad([DAMPING / (r + 6.0) for r in react0])
    scale1 = broad([DAMPING / (r + 6.0 * 0.25) for r in react1])
    scale2 = [DAMPING / (r + 6.0 * 0.0625) for r in react2]

    all_of(gather_y, on_y, 0).wait_recv()
    for j in range(n_y):
        block[j : j + 1, :] = gather_y[j, 0:1, :]
    summed = jnp.sum(gather_y[...], axis=0)
    block[4:7, :] = summed[1:4]
    block[7:8, :] = summed[0:1]
    gather[at_z] = block[...]
    send_all(block, gather.at[at_z], on_z, 1)

    for copy in faces:
        copy.wait_recv()
    under = natural([[halo[d, c] for c in range(3)] for d in range(3)], 0)
    source = own_faces - under
    base = join(local_solve(split(source), diag0, scale0, scale1, scale2))

    all_of(gather, on_z, 1).wait_recv()
    loads[5].wait()
    rows_y = n_sub // DOM_Z
    lane_a = iota((rows_y, 128), 1)
    quads = []
    for b in range(DOM_Z):
        places = [(DOM_Z * (a % 2) + b, a // 2) for a in range(rows_y)]
        quads.append(jnp.concatenate([gather[i, j : j + 1, :] for i, j in places], axis=0))

    def shifted(v, by):
        return pltpu.roll(v, by % 128, 1) if by % 128 else v

    packed = [
        jnp.where(lane_a < 96, quads[0], shifted(quads[1], 96)),
        jnp.where(lane_a < 64, shifted(quads[1], -32), shifted(quads[2], 64)),
        jnp.where(lane_a < 32, shifted(quads[2], -64), shifted(quads[3], 32)),
    ]
    lanes = jnp.zeros((96, 128), F32)
    for a in range(rows_y):
        for j in range(3):
            at = (3 * a + j) * 128
            lanes = lanes + v_rows[0, :, at : at + 128] * packed[j][a : a + 1, :]

    def lane_total(v):
        tall = jnp.concatenate([v, jnp.zeros((32, 128), F32)], axis=0)
        return jnp.sum(jnp.transpose(tall), axis=0, keepdims=True)

    region_row = lane_total(lanes)
    part = jnp.sum(source * base, axis=0, keepdims=True)
    part = part[:, :128] + part[:, 128:] + primal_row * region_row
    packet3[...] = part
    place = region * n_sub + sub
    gather3[place] = part
    send_all(packet3, gather3.at[place], everyone, 3)

    packet2[...] = jnp.sum(gather[...], axis=0)[4:8]
    gather2[region] = packet2[...]
    send_all(packet2, gather2.at[region], on_region, 2)

    def extract(edge):
        mask_y = tile3(y_lane == edge)
        mask_z = tile3(z_lane == edge)
        in_y = collect(exact_dot(jnp.where(mask_y, base, 0.0), table[same]))
        in_z = collect(exact_dot(jnp.where(mask_z, base, 0.0), table[from_z]))
        in_x = [base[CELLS * c + edge : CELLS * c + edge + 1] for c in range(3)]
        return [in_x, in_y, in_z]

    lower_rows = extract(0)
    for d in range(3):
        for c in range(3):
            face_send[d, c] = lower_rows[d][c]
    backs = [
        pltpu.make_async_remote_copy(
            src_ref=face_send.at[d],
            dst_ref=after.at[d],
            send_sem=back_send.at[d],
            recv_sem=back_recv.at[d],
            device_id=below[d],
            device_id_type=MESH,
        )
        for d in (1, 2, 0)
    ]
    for copy in backs:
        copy.start()

    all_of(gather2, on_region, 2).wait_recv()
    whole = jnp.sum(gather2[...], axis=0)
    squares_all = jnp.sum(jnp.where(lane_row == 96, whole[3:4, :], 0.0))
    total = jnp.concatenate([whole[0:1, :], whole[1:2, :], whole[2:3, :]], axis=1)
    loads[6].wait()
    top = lax.dot_general(
        jnp.broadcast_to(total, (8, 384)),
        v_ginv[...],
        (((1,), (1,)), ((), ())),
        precision=lax.Precision.HIGHEST,
        preferred_element_type=F32,
    )[0:1]
    energy = jnp.sum(total * top)
    weighted = v_map[0] * top
    lanes = weighted[:, :128] + weighted[:, 128:256] + weighted[:, 256:]
    lifted = region_row + lane_total(lanes)
    key_row = jnp.broadcast_to(index_row >> 7, (32, 128))
    placed = jnp.where(key_row == iota((32, 128), 0), jnp.broadcast_to(lifted, (32, 128)), 0.0)
    placed = exact_dot(placed, hit.astype(BF16))

    def lifted_row(d, c):
        r = (d * 3 + c) * 2
        return jnp.concatenate([placed[r : r + 1], placed[r + 1 : r + 2]], axis=1)

    lifted_rows = [[lifted_row(d, c) for c in range(3)] for d in range(3)]
    field = base + natural(lifted_rows, upper)
    upper_rows = extract(upper)
    for c in range(3):
        velocity[0, c] = field[CELLS * c : CELLS * c + CELLS]

    for copy in backs:
        copy.wait_recv()
    loads[7].wait()
    v = [field[CELLS * c : CELLS * c + CELLS] for c in range(3)]
    edge_x = jnp.broadcast_to(after[0, 0], (CELLS, FACE))
    edge_y = exact_dot(spread([after[1, 1]]), table[same])
    edge_z = exact_dot(spread([after[2, 2]]), table[to_z])
    step_x = jnp.where(x_row == upper, edge_x, pltpu.roll(v[0], CELLS - 1, 0)) - v[0]
    step_y = jnp.where(y_lane == upper, edge_y, pltpu.roll(v[1], FACE - CELLS, 1)) - v[1]
    step_z = jnp.where(z_lane == upper, edge_z, pltpu.roll(v[2], FACE - 1, 1)) - v[2]
    pressure[0] = -v_visc[0] * (step_x + step_y + step_z)
    for d in range(3):
        for c in range(3):
            jump[d, c] = upper_rows[d][c] + lifted_rows[d][c] - after[d, c]

    all_of(gather3, everyone, 3).wait_recv()
    curvature = jnp.sum(gather3[...]) + energy
    alpha[...] = jnp.broadcast_to(squares_all / curvature, (8, 128))

    for copy in faces + backs:
        copy.wait_send()
    all_of(gather_y, on_y, 0).wait_send()
    all_of(gather, on_z, 1).wait_send()
    all_of(gather2, on_region, 2).wait_send()
    all_of(gather3, everyone, 3).wait_send()


def finish(multipliers, direction, residual, jump, alpha, velocity, pressure, *outs):
    step = jnp.broadcast_to(alpha[0:1, 0:1], (1, FACE))
    for d in range(3):
        for c in range(3):
            outs[0][d, c] = multipliers[d, c] + step * direction[d, c]
            outs[1][d, c] = residual[d, c] - step * jump[d, c]
    outs[2][...] = velocity[...]
    outs[3][...] = pressure[...]


def solution(mesh):
    n_region = mesh.shape["region"]
    n_sub = mesh.shape["sub"]

    def body(multipliers, direction, residual, *rest):
        faces = [a.reshape(3, 3, 1, FACE) for a in (multipliers, direction, residual)]
        args = [pltpu.with_memory_space_constraint(a, pltpu.HBM) for a in (faces[1], faces[2]) + rest]
        face = jax.ShapeDtypeStruct((3, 3, 1, FACE), F32)
        cells = jax.ShapeDtypeStruct((1, 3, CELLS, FACE), F32)
        scalar_cells = jax.ShapeDtypeStruct((1, CELLS, FACE), F32)
        inner = pl.pallas_call(
            functools.partial(kernel, n_region, n_sub),
            out_shape=[face, jax.ShapeDtypeStruct((8, 128), F32), cells, scalar_cells],
            in_specs=[pl.BlockSpec(memory_space=pltpu.HBM)] * 8,
            out_specs=[pl.BlockSpec(memory_space=pltpu.VMEM)] * 4,
            scratch_shapes=[pltpu.VMEM(a.shape, a.dtype) for a in args]
            + [
                pltpu.VMEM((3, FACE, FACE), BF16),
                pltpu.VMEM((8, 128), jnp.int32),
                pltpu.VMEM((3, 3, 1, FACE), F32),
                pltpu.VMEM((3, 3, 1, FACE), F32),
                pltpu.VMEM((3, 3, 1, FACE), F32),
                pltpu.VMEM((4, 128), F32),
                pltpu.VMEM((n_sub // Z_LINE, 4, 128), F32),
                pltpu.VMEM((8, 128), F32),
                pltpu.VMEM((Z_LINE, 8, 128), F32),
                pltpu.VMEM((4, 128), F32),
                pltpu.VMEM((n_region, 4, 128), F32),
                pltpu.VMEM((1, 128), F32),
                pltpu.VMEM((n_region * n_sub, 1, 128), F32),
                pltpu.SemaphoreType.DMA((8,)),
                pltpu.SemaphoreType.DMA((3,)),
                pltpu.SemaphoreType.DMA((3,)),
                pltpu.SemaphoreType.DMA((3,)),
                pltpu.SemaphoreType.DMA((3,)),
                pltpu.SemaphoreType.DMA((4,)),
                pltpu.SemaphoreType.DMA((4,)),
            ],
            compiler_params=pltpu.CompilerParams(
                collective_id=0, has_side_effects=True, vmem_limit_bytes=VMEM_LIMIT
            ),
            name="feti",
        )
        jump, alpha, velocity, pressure = inner(*args)
        outs = pl.pallas_call(
            finish,
            out_shape=[face, face, cells, scalar_cells],
            in_specs=[pl.BlockSpec(memory_space=pltpu.VMEM)] * 7,
            out_specs=[pl.BlockSpec(memory_space=pltpu.VMEM)] * 4,
            compiler_params=pltpu.CompilerParams(vmem_limit_bytes=VMEM_LIMIT),
            name="finish",
        )(*faces, jump, alpha, velocity, pressure)
        shape = multipliers.shape
        return outs[0].reshape(shape), outs[1].reshape(shape), outs[2], outs[3]

    in_specs = (
        P(("region", "sub"), None, None, None),
        P(("region", "sub"), None, None, None),
        P(("region", "sub"), None, None, None),
        P(("region", "sub"), None, None),
        P(("region", "sub"), None, None),
        P(("region", "sub"), None),
        P("region", "sub", None),
        P(("region", "sub"), None, None),
        P(),
    )
    out_specs = (
        P(("region", "sub"), None, None, None),
        P(("region", "sub"), None, None, None),
        P(("region", "sub"), None, None, None),
        P(("region", "sub"), None, None),
    )
    return jax.shard_map(body, mesh=mesh, in_specs=in_specs, out_specs=out_specs, check_vma=False)
```

```python
import functools

import jax
import jax.numpy as jnp
from jax import lax
from jax.experimental import pallas as pl
from jax.experimental.pallas import tpu as pltpu
from jax.sharding import PartitionSpec as P

DOM_Z = 4
Z_LINE = 8
COARSE_SWEEPS = 8
CELLS = 16
FACE = 256
DAMPING = 0.8
VMEM_LIMIT = 16 * 1024 * 1024
KEEP = 0.2
MESH = pl.DeviceIdType.MESH
F32 = jnp.float32
BF16 = jnp.bfloat16


def roll(v, by, axis):
    return pltpu.roll(v, by % v.shape[axis], axis)


def flag(condition):
    return jnp.where(condition, 1.0, 0.0)


def iota(shape, axis):
    return lax.broadcasted_iota(jnp.int32, shape, axis)


def split(field):
    lead = field.shape[0] // CELLS
    cubic = field.reshape(lead, CELLS, FACE)
    return [cubic[:, 8 * i : 8 * i + 8, 128 * j : 128 * j + 128] for i in (0, 1) for j in (0, 1)]


def join(parts):
    low = jnp.concatenate([parts[0], parts[1]], axis=2)
    high = jnp.concatenate([parts[2], parts[3]], axis=2)
    whole = jnp.concatenate([low, high], axis=1)
    return whole.reshape(whole.shape[0] * CELLS, FACE)


def neighbours(parts, step):
    shape = parts[0].shape
    x = iota(shape, 1)
    lane = iota(shape, 2)
    y = lane >> 4
    z = lane & 15

    sums = []
    ys_up = [roll(v, 16 * step, 2) for v in parts]
    ys_down = ys_up if step == 4 else [roll(v, -16 * step, 2) for v in parts]
    xs_up = [roll(v, step, 1) for v in parts]
    xs_down = xs_up if step == 4 else [roll(v, -step, 1) for v in parts]
    for i in (0, 1):
        for j in (0, 1):
            k = 2 * i + j
            v = parts[k]
            total = jnp.where(z >= step, roll(v, step, 2), 0.0)
            total = total + jnp.where(z < CELLS - step, roll(v, -step, 2), 0.0)
            before = ys_up[k - 1] if j == 1 else 0.0
            total = total + jnp.where(y >= step, ys_up[k], before)
            after = ys_down[k + 1] if j == 0 else 0.0
            total = total + jnp.where(y < 8 - step, ys_down[k], after)
            before = xs_up[k - 2] if i == 1 else 0.0
            total = total + jnp.where(x >= step, xs_up[k], before)
            after = xs_down[k + 2] if i == 0 else 0.0
            total = total + jnp.where(x < 8 - step, xs_down[k], after)
            sums.append(total)
    return sums


def block_mean(parts, step):
    shape = parts[0].shape
    x = iota(shape, 1)
    lane = iota(shape, 2)

    def pair(v, by, axis, even):
        count = v.shape[axis]
        return v + jnp.where(even, pltpu.roll(v, count - by, axis), pltpu.roll(v, by, axis))

    result = []
    for v in parts:
        v = pair(v, step, 2, (lane & step) == 0)
        v = pair(v, 16 * step, 2, ((lane >> 4) & step) == 0)
        v = pair(v, step, 1, (x & step) == 0)
        result.append(v * 0.125)
    return result


def merge(parts):
    spot = iota(parts[0].shape[1:], 1) & 3
    return [jnp.where(spot == 0, v[0], jnp.where(spot == 1, v[1], v[2]))[None] for v in parts]


def unmerge(parts):
    result = []
    for v in parts:
        v = v[0]
        spot = iota(v.shape, 1) & 3
        moved = {by: pltpu.roll(v, by % 128, 1) if by else v for by in range(-2, 4)}
        comps = []
        for c in range(3):
            value = moved[3 - c]
            for t in (2, 1, 0):
                value = jnp.where(spot == t, moved[t - c], value)
            comps.append(value)
        result.append(jnp.stack(comps, axis=0))
    return result


def broad(parts):
    return [jnp.broadcast_to(v, (3,) + v.shape[1:]) for v in parts]


def coarse_weights(scale2):
    shape = scale2[0].shape
    x = iota(shape, 1)
    y = iota(shape, 2) >> 4
    z = iota(shape, 2) & 15
    result = []
    for k, w in enumerate(scale2):
        near = w * 0.0625
        other_y = flag(y < 4) if k & 1 else flag(y >= 4)
        other_x = flag(x < 4) if k & 2 else flag(x >= 4)
        result.append((near, near * flag(z >= 4), near * flag(z < 12), near * other_y, near * other_x))
    return result


def coarse_solve(source, scale2, weights):
    wb = [w * s for w, s in zip(scale2, merge(source))]
    v = wb
    for _ in range(COARSE_SWEEPS - 1):
        along_y = [roll(a, 64, 2) for a in v]
        along_x = [roll(a, 4, 1) for a in v]
        new = []
        for k, (near, low, high, other_y, other_x) in enumerate(weights):
            total = (KEEP * v[k] + wb[k]) + near * (along_y[k] + along_x[k])
            total = total + (other_y * along_y[k ^ 1] + other_x * along_x[k ^ 2])
            new.append(total + (low * roll(v[k], 4, 2) + high * roll(v[k], -4, 2)))
        v = new
    return unmerge(v)


def middle_solve(source, scale1, scale2, weights, meanwhile):
    wb = [w * s for w, s in zip(scale1, source)]
    near = neighbours(wb, 2)
    remain = [KEEP * s + 0.25 * n for s, n in zip(source, near)]
    coarse = coarse_solve(block_mean(remain, 2), scale2, weights)
    v = [a + c for a, c in zip(wb, coarse)]
    near = neighbours(v, 2)
    return [KEEP * a + (c + (w * 0.25) * n) for a, c, w, n in zip(v, wb, scale1, near)]


def local_solve(source, diag0, scale0, scale1, scale2, weights, meanwhile):
    wb = [w * s for w, s in zip(scale0, source)]
    v = None
    for cycle in range(2):
        if cycle == 0:
            v = wb
            remain = [KEEP * s + n for s, n in zip(source, neighbours(v, 1))]
        else:
            near = neighbours(v, 1)
            v = [KEEP * a + (c + w * n) for a, c, w, n in zip(v, wb, scale0, near)]
            near = neighbours(v, 1)
            remain = [(s - d * a) + n for s, d, a, n in zip(source, diag0, v, near)]
        hook = meanwhile if cycle else lambda: None
        coarse = middle_solve(block_mean(remain, 1), scale1, scale2, weights, hook)
        v = [a + c for a, c in zip(v, coarse)]
        hook()
        near = neighbours(v, 1)
        v = [KEEP * a + (c + w * n) for a, c, w, n in zip(v, wb, scale0, near)]
    return v


def exact_dot(left, right):
    high = left.astype(BF16)
    rest = left - high.astype(F32)
    mid = rest.astype(BF16)
    low = (rest - mid.astype(F32)).astype(BF16)
    dot = functools.partial(jnp.dot, preferred_element_type=F32)
    return dot(high, right) + (dot(mid, right) + dot(low, right))


def spread(rows):
    own = (iota((8, 128), 1) >> 4) == iota((8, 128), 0)
    tiles = [jnp.where(own, jnp.broadcast_to(r[:, h : h + 128], (8, 128)), 0.0) for r in rows for h in (0, 128)]
    return jnp.concatenate(tiles, axis=0)


def collect(field):
    own = (iota((8, 128), 1) >> 4) == iota((8, 128), 0)
    tiles = [
        jnp.sum(jnp.where(own, field[8 * i : 8 * i + 8], 0.0), axis=0, keepdims=True) for i in range(6)
    ]
    return [jnp.concatenate(tiles[2 * c : 2 * c + 2], axis=1) for c in range(3)]


def kernel(
    n_region,
    n_sub,
    direction,
    residual,
    reaction,
    viscosity,
    primal_index,
    region_inverse,
    coarse_map,
    global_inverse,
    jump,
    alpha,
    velocity,
    pressure,
    v_dir,
    v_res,
    v_react,
    v_visc,
    v_index,
    v_rows,
    v_map,
    v_ginv,
    table_y,
    table_z,
    table_back,
    padded_index,
    halo,
    face_send,
    after,
    packet,
    gather_y,
    gather,
    block_sums,
    gather_sums,
    packet2,
    gather2,
    packet3,
    gather3,
    sent_rows,
    load_sem,
    halo_send,
    halo_recv,
    back_send,
    back_recv,
    sum_send,
    sum_recv,
):
    region = lax.axis_index("region")
    sub = lax.axis_index("sub")

    n_y = n_sub // Z_LINE
    at_y = sub >> (Z_LINE.bit_length() - 1)
    at_z = sub & (Z_LINE - 1)

    def sub_peer(i):
        return (region, (sub + i) & (n_sub - 1))

    def region_peer(i):
        return ((region + i) & (n_region - 1), sub)

    def y_peer(i):
        return (region, ((at_y + i) & (n_y - 1)) * Z_LINE + at_z)

    def z_peer(i):
        return (region, at_y * Z_LINE + ((at_z + i) & (Z_LINE - 1)))

    barrier = pltpu.get_barrier_semaphore()

    def hops_of(i):
        carry = [min(j, n_y - j) for j in (i // Z_LINE, (i // Z_LINE + 1) % n_y)]
        return max(carry) + min(i % Z_LINE, Z_LINE - i % Z_LINE)

    urgent = [n_sub - DOM_Z, n_sub - 1, DOM_Z, 1]
    others = sorted((i for i in range(1, n_sub) if i not in urgent), key=lambda i: -hops_of(i))
    near = [sub_peer(i) for i in urgent] + [region_peer(n_region - 1), region_peer(1)]
    on_sub = [sub_peer(i) for i in others + urgent]
    near += [sub_peer(i) for i in others] + [region_peer(i) for i in range(2, n_region - 1)]
    for peer in near:
        pl.semaphore_signal(barrier, inc=1, device_id=peer, device_id_type=MESH)

    loads = [
        pltpu.make_async_copy(src, dst, load_sem.at[i])
        for i, (src, dst) in enumerate(
            (
                (direction, v_dir),
                (primal_index, v_index),
                (coarse_map, v_map),
                (residual, v_res),
                (reaction, v_react),
                (region_inverse, v_rows),
                (global_inverse, v_ginv),
                (viscosity, v_visc),
            )
        )
    ]
    for load in loads:
        load.start()

    def send_all(src, dst_of_me, peers, index):
        for peer in peers:
            pltpu.make_async_remote_copy(
                src_ref=src,
                dst_ref=dst_of_me,
                send_sem=sum_send.at[index],
                recv_sem=sum_recv.at[index],
                device_id=peer,
                device_id_type=MESH,
            ).start()

    def all_of(buffer, peers, index):
        part = buffer.at[pl.ds(0, len(peers))] if peers else buffer
        return pltpu.make_async_remote_copy(
            src_ref=part,
            dst_ref=part,
            send_sem=sum_send.at[index],
            recv_sem=sum_recv.at[index],
            device_id=(peers or on_y)[0],
            device_id_type=MESH,
        )

    on_y = [y_peer(i) for i in range(1, n_y)]
    on_z = [z_peer(i) for i in range(1, Z_LINE)]
    on_region = [region_peer(i) for i in range(1, n_region)]

    at_x = region >> 1
    at_c = region & 1
    n_x = n_region // 2
    found = []
    for dx in range(n_x):
        for dc in range(2):
            for dy in range(n_y):
                for dz in range(Z_LINE):
                    if dx or dc or dy or dz:
                        hops = min(dx, n_x - dx) + min(dy, n_y - dy) + min(dz, Z_LINE - dz)
                        found.append((-hops, dx, dc, dy, dz))
    found.sort()
    xs = [((at_x + i) & (n_x - 1)) * 2 for i in range(n_x)]
    cs = [(at_c + i) & 1 for i in range(2)]
    ys = [((at_y + i) & (n_y - 1)) * Z_LINE for i in range(n_y)]
    zs = [((at_z + i) & (Z_LINE - 1)) for i in range(Z_LINE)]
    everyone = [(xs[dx] + cs[dc], ys[dy] + zs[dz]) for _, dx, dc, dy, dz in found]

    loads[0].wait()
    loads[1].wait()
    padded_index[...] = jnp.full((8, 128), -1, jnp.int32)
    padded_index[0:1, 0:96] = v_index[...]
    index_row = padded_index[0:1, :]
    index_col = jnp.transpose(jnp.broadcast_to(index_row.astype(F32), (128, 128))).astype(jnp.int32)
    lane128 = iota((128, 128), 1)
    hit = jnp.where((index_col & 127) == lane128, 1.0, 0.0)
    key_col = index_col >> 7
    picked = jnp.zeros((128, 128), F32)
    for d in range(3):
        for c in range(3):
            for h in range(2):
                r = (d * 3 + c) * 2 + h
                values = v_dir[d, c, :, 128 * h : 128 * h + 128]
                picked = jnp.where(key_col == r, jnp.broadcast_to(values, (128, 128)), picked)
    picked = picked * hit
    primal_row = jnp.sum(jnp.transpose(picked), axis=0, keepdims=True)
    primal_col = jnp.sum(picked, axis=1, keepdims=True)[:96]
    loads[2].wait()
    share = jnp.sum(primal_col * v_map[0], axis=0, keepdims=True)
    loads[3].wait()
    squares = jnp.sum(v_res[...] * v_res[...])
    lane_row = iota((1, 128), 1)
    packet[0:1, :] = jnp.where(lane_row < 96, primal_row, squares)
    for j in range(3):
        packet[j + 1 : j + 2, :] = share[:, 128 * j : 128 * j + 128]
    gather_y[at_y] = packet[...]
    gather[sub] = packet[0:1, :]

    pl.semaphore_wait(barrier, len(near))

    def face_copy(src, dst, send, recv, peer):
        return pltpu.make_async_remote_copy(
            src_ref=src, dst_ref=dst, send_sem=send, recv_sem=recv, device_id=peer, device_id_type=MESH
        )

    below = (region_peer(n_region - 1), sub_peer(n_sub - DOM_Z), sub_peer(n_sub - 1))
    faces = [
        face_copy(v_dir.at[1], halo.at[1], halo_send.at[1], halo_recv.at[1], sub_peer(DOM_Z)),
        face_copy(v_dir.at[2], halo.at[2], halo_send.at[2], halo_recv.at[2], sub_peer(1)),
        face_copy(v_dir.at[0], halo.at[0], halo_send.at[0], halo_recv.at[0], region_peer(1)),
    ]
    for copy in faces:
        copy.start()
    send_all(packet.at[pl.ds(0, 1)], gather.at[sub], on_sub, 1)
    send_all(packet, gather_y.at[at_y], on_y, 0)
    row_i = iota((128, FACE), 0)
    col_i = iota((128, FACE), 1)
    to_y = jnp.where((row_i[:, :128] & 15) == (col_i[:, :128] & 15), 1.0, 0.0).astype(BF16)
    to_z = jnp.where((row_i & 15) == (col_i >> 4), 1.0, 0.0).astype(BF16)
    table_y[...] = to_y
    table_z[...] = to_z
    row_i = iota((FACE, 128), 0)
    col_i = iota((FACE, 128), 1)
    table_back[...] = jnp.where((row_i >> 4) == (col_i & 15), 1.0, 0.0).astype(BF16)
    lane = iota((CELLS, FACE), 1)
    y_lane = lane >> 4
    z_lane = lane & 15
    x_row = iota((CELLS, FACE), 0)

    def tile3(mask):
        return jnp.concatenate([mask] * 3, axis=0)

    def natural(face_rows, edge):
        in_y = exact_dot(spread(face_rows[1]), table_y[...])
        in_z = exact_dot(spread(face_rows[2]), table_z[...])
        blocks = []
        for c in range(3):
            rows = slice(CELLS * c, CELLS * c + CELLS)
            both = jnp.concatenate([in_y[rows], in_y[rows]], axis=1)
            part = jnp.where(x_row == edge, jnp.broadcast_to(face_rows[0][c], (CELLS, FACE)), 0.0)
            part = part + jnp.where(y_lane == edge, both, 0.0)
            part = part + jnp.where(z_lane == edge, in_z[rows], 0.0)
            blocks.append(part)
        return jnp.concatenate(blocks, axis=0)

    upper = CELLS - 1
    own_faces = natural([[v_dir[d, c] for c in range(3)] for d in range(3)], upper)
    loads[4].wait()
    react0 = split(v_react[0])
    react1 = block_mean(react0, 1)
    react2 = block_mean(react1, 2)
    diag0 = broad([r + 6.0 for r in react0])
    scale0 = broad([DAMPING / (r + 6.0) for r in react0])
    scale1 = broad([DAMPING / (r + 6.0 * 0.25) for r in react1])
    scale2 = [DAMPING / (r + 6.0 * 0.0625) for r in react2]
    weights = coarse_weights(scale2)

    all_of(gather_y, on_y, 0).wait_recv()
    summed = jnp.sum(gather_y[...], axis=0)
    block_sums[0:3, :] = summed[1:4]
    block_sums[3:4, :] = summed[0:1]
    gather_sums[at_z] = block_sums[...]
    send_all(block_sums, gather_sums.at[at_z], on_z, 4)

    def lane_total(v):
        tall = jnp.concatenate([v, jnp.zeros((32, 128), F32)], axis=0)
        return jnp.sum(jnp.transpose(tall), axis=0, keepdims=True)

    region_lanes = []

    def region_operator():
        all_of(gather, on_sub, 1).wait_recv()
        loads[5].wait()
        rows_y = n_sub // DOM_Z
        lane_a = iota((rows_y, 128), 1)
        quads = []
        for b in range(DOM_Z):
            quads.append(jnp.concatenate([gather[DOM_Z * a + b] for a in range(rows_y)], axis=0))

        def shifted(v, by):
            return pltpu.roll(v, by % 128, 1) if by % 128 else v

        packed = [
            jnp.where(lane_a < 96, quads[0], shifted(quads[1], 96)),
            jnp.where(lane_a < 64, shifted(quads[1], -32), shifted(quads[2], 64)),
            jnp.where(lane_a < 32, shifted(quads[2], -64), shifted(quads[3], 32)),
        ]
        lanes = jnp.zeros((96, 128), F32)
        for a in range(rows_y):
            for j in range(3):
                at = (3 * a + j) * 128
                lanes = lanes + v_rows[0, :, at : at + 128] * packed[j][a : a + 1, :]

        region_lanes.append(lanes)

    for copy in faces:
        copy.wait_recv()
    under = natural([[halo[d, c] for c in range(3)] for d in range(3)], 0)
    source = own_faces - under
    base = join(local_solve(split(source), diag0, scale0, scale1, scale2, weights, region_operator))

    part = jnp.sum(source * base, axis=0, keepdims=True)
    part = part[:, :128] + part[:, 128:] + jnp.sum(primal_col * region_lanes[0], axis=0, keepdims=True)
    packet3[...] = part
    place = region * n_sub + sub
    mine = gather3.at[place >> 3, pl.ds(place & 7, 1)]
    send_all(packet3, mine, everyone, 3)
    pltpu.make_async_copy(packet3, mine, sum_recv.at[3]).start()

    all_of(gather_sums, on_z, 4).wait_recv()
    packet2[...] = jnp.sum(gather_sums[...], axis=0)
    gather2[region] = packet2[...]
    send_all(packet2, gather2.at[region], on_region, 2)

    def extract(edge):
        half = 128 if edge else 0
        at_edge = (iota((3 * CELLS, 128), 1) >> 4) == (edge & 7)
        in_y = collect(exact_dot(jnp.where(at_edge, base[:, half : half + 128], 0.0), table_y[...]))
        in_z = collect(exact_dot(jnp.where(tile3(z_lane == edge), base, 0.0), table_back[...]))
        in_x = [base[CELLS * c + edge : CELLS * c + edge + 1] for c in range(3)]
        return [in_x, in_y, in_z]

    lower_rows = extract(0)
    for d in range(3):
        for c in range(3):
            face_send[d, c] = lower_rows[d][c]
    backs = [
        pltpu.make_async_remote_copy(
            src_ref=face_send.at[d],
            dst_ref=after.at[d],
            send_sem=back_send.at[d],
            recv_sem=back_recv.at[d],
            device_id=below[d],
            device_id_type=MESH,
        )
        for d in (1, 2, 0)
    ]
    for copy in backs:
        copy.start()

    all_of(gather2, on_region, 2).wait_recv()
    whole = jnp.sum(gather2[...], axis=0)
    squares_all = jnp.sum(jnp.where(lane_row == 96, whole[3:4, :], 0.0))
    total = jnp.concatenate([whole[0:1, :], whole[1:2, :], whole[2:3, :]], axis=1)
    loads[6].wait()
    top = lax.dot_general(
        jnp.broadcast_to(total, (8, 384)),
        v_ginv[...],
        (((1,), (1,)), ((), ())),
        precision=lax.Precision.HIGHEST,
        preferred_element_type=F32,
    )[0:1]
    energy = jnp.sum(total * top)
    weighted = v_map[0] * top
    lanes = weighted[:, :128] + weighted[:, 128:256] + weighted[:, 256:]
    lifted = lane_total(region_lanes[0] + lanes)
    key_row = jnp.broadcast_to(index_row >> 7, (32, 128))
    placed = jnp.where(key_row == iota((32, 128), 0), jnp.broadcast_to(lifted, (32, 128)), 0.0)
    placed = exact_dot(placed, hit.astype(BF16))

    def lifted_row(d, c):
        r = (d * 3 + c) * 2
        return jnp.concatenate([placed[r : r + 1], placed[r + 1 : r + 2]], axis=1)

    lifted_rows = [[lifted_row(d, c) for c in range(3)] for d in range(3)]
    field = base + natural(lifted_rows, upper)
    upper_rows = extract(upper)
    for c in range(3):
        velocity[0, c] = field[CELLS * c : CELLS * c + CELLS]

    for copy in backs:
        copy.wait_recv()
    loads[7].wait()
    v = [field[CELLS * c : CELLS * c + CELLS] for c in range(3)]
    edge_x = jnp.broadcast_to(after[0, 0], (CELLS, FACE))
    edge_y = exact_dot(spread([after[1, 1]]), table_y[...])
    edge_y = jnp.concatenate([edge_y, edge_y], axis=1)
    edge_z = exact_dot(spread([after[2, 2]]), table_z[...])
    step_x = jnp.where(x_row == upper, edge_x, pltpu.roll(v[0], CELLS - 1, 0)) - v[0]
    step_y = jnp.where(y_lane == upper, edge_y, pltpu.roll(v[1], FACE - CELLS, 1)) - v[1]
    step_z = jnp.where(z_lane == upper, edge_z, pltpu.roll(v[2], FACE - 1, 1)) - v[2]
    pressure[0] = -v_visc[0] * (step_x + step_y + step_z)
    for d in range(3):
        for c in range(3):
            jump[d, c] = upper_rows[d][c] + lifted_rows[d][c] - after[d, c]

    all_of(gather3, None, 3).wait_recv()
    curvature = jnp.sum(gather3[...]) + energy
    alpha[...] = jnp.broadcast_to(squares_all / curvature, (8, 128))

    for copy in faces + backs:
        copy.wait_send()
    all_of(gather_y, on_y, 0).wait_send()
    all_of(gather, on_sub, 1).wait_send()
    all_of(gather_sums, on_z, 4).wait_send()
    all_of(gather2, on_region, 2).wait_send()
    all_of(sent_rows, None, 3).wait_send()


def finish(multipliers, direction, residual, jump, alpha, velocity, pressure, *outs):
    step = jnp.broadcast_to(alpha[0:1, 0:1], (1, FACE))
    for d in range(3):
        for c in range(3):
            outs[0][d, c] = multipliers[d, c] + step * direction[d, c]
            outs[1][d, c] = residual[d, c] - step * jump[d, c]
    outs[2][...] = velocity[...]
    outs[3][...] = pressure[...]


def solution(mesh):
    n_region = mesh.shape["region"]
    n_sub = mesh.shape["sub"]

    def body(multipliers, direction, residual, *rest):
        faces = [a.reshape(3, 3, 1, FACE) for a in (multipliers, direction, residual)]
        args = [pltpu.with_memory_space_constraint(a, pltpu.HBM) for a in (faces[1], faces[2]) + rest]
        face = jax.ShapeDtypeStruct((3, 3, 1, FACE), F32)
        cells = jax.ShapeDtypeStruct((1, 3, CELLS, FACE), F32)
        scalar_cells = jax.ShapeDtypeStruct((1, CELLS, FACE), F32)
        inner = pl.pallas_call(
            functools.partial(kernel, n_region, n_sub),
            out_shape=[face, jax.ShapeDtypeStruct((8, 128), F32), cells, scalar_cells],
            in_specs=[pl.BlockSpec(memory_space=pltpu.HBM)] * 8,
            out_specs=[pl.BlockSpec(memory_space=pltpu.VMEM)] * 4,
            scratch_shapes=[pltpu.VMEM(a.shape, a.dtype) for a in args]
            + [
                pltpu.VMEM((128, 128), BF16),
                pltpu.VMEM((128, FACE), BF16),
                pltpu.VMEM((FACE, 128), BF16),
                pltpu.VMEM((8, 128), jnp.int32),
                pltpu.VMEM((3, 3, 1, FACE), F32),
                pltpu.VMEM((3, 3, 1, FACE), F32),
                pltpu.VMEM((3, 3, 1, FACE), F32),
                pltpu.VMEM((4, 128), F32),
                pltpu.VMEM((n_sub // Z_LINE, 4, 128), F32),
                pltpu.VMEM((n_sub, 1, 128), F32),
                pltpu.VMEM((4, 128), F32),
                pltpu.VMEM((Z_LINE, 4, 128), F32),
                pltpu.VMEM((4, 128), F32),
                pltpu.VMEM((n_region, 4, 128), F32),
                pltpu.VMEM((1, 128), F32),
                pltpu.VMEM((n_region * n_sub // 8, 8, 128), F32),
                pltpu.VMEM((n_region * n_sub - 1, 1, 128), F32),
                pltpu.SemaphoreType.DMA((8,)),
                pltpu.SemaphoreType.DMA((3,)),
                pltpu.SemaphoreType.DMA((3,)),
                pltpu.SemaphoreType.DMA((3,)),
                pltpu.SemaphoreType.DMA((3,)),
                pltpu.SemaphoreType.DMA((5,)),
                pltpu.SemaphoreType.DMA((5,)),
            ],
            compiler_params=pltpu.CompilerParams(
                collective_id=0, has_side_effects=True, vmem_limit_bytes=VMEM_LIMIT
            ),
            name="feti",
        )
        jump, alpha, velocity, pressure = inner(*args)
        outs = pl.pallas_call(
            finish,
            out_shape=[face, face, cells, scalar_cells],
            in_specs=[pl.BlockSpec(memory_space=pltpu.VMEM)] * 7,
            out_specs=[pl.BlockSpec(memory_space=pltpu.VMEM)] * 4,
            compiler_params=pltpu.CompilerParams(vmem_limit_bytes=VMEM_LIMIT),
            name="finish",
        )(*faces, jump, alpha, velocity, pressure)
        shape = multipliers.shape
        return outs[0].reshape(shape), outs[1].reshape(shape), outs[2], outs[3]

    in_specs = (
        P(("region", "sub"), None, None, None),
        P(("region", "sub"), None, None, None),
        P(("region", "sub"), None, None, None),
        P(("region", "sub"), None, None),
        P(("region", "sub"), None, None),
        P(("region", "sub"), None),
        P("region", "sub", None),
        P(("region", "sub"), None, None),
        P(),
    )
    out_specs = (
        P(("region", "sub"), None, None, None),
        P(("region", "sub"), None, None, None),
        P(("region", "sub"), None, None, None),
        P(("region", "sub"), None, None),
    )
    return jax.shard_map(body, mesh=mesh, in_specs=in_specs, out_specs=out_specs, check_vma=False)
```

```python
import functools

import jax
import jax.numpy as jnp
from jax import lax
from jax.experimental import pallas as pl
from jax.experimental.pallas import tpu as pltpu
from jax.sharding import PartitionSpec as P

DOM_Z = 4
Z_LINE = 8
COARSE_SWEEPS = 8
CELLS = 16
FACE = 256
DAMPING = 0.8
VMEM_LIMIT = 16 * 1024 * 1024
KEEP = 0.2
MESH = pl.DeviceIdType.MESH
F32 = jnp.float32
BF16 = jnp.bfloat16


def roll(v, by, axis):
    return pltpu.roll(v, by % v.shape[axis], axis)


def flag(condition):
    return jnp.where(condition, 1.0, 0.0)


def iota(shape, axis):
    return lax.broadcasted_iota(jnp.int32, shape, axis)


def split(field):
    lead = field.shape[0] // CELLS
    cubic = field.reshape(lead, CELLS, FACE)
    return [cubic[:, 8 * i : 8 * i + 8, 128 * j : 128 * j + 128] for i in (0, 1) for j in (0, 1)]


def join(parts):
    low = jnp.concatenate([parts[0], parts[1]], axis=2)
    high = jnp.concatenate([parts[2], parts[3]], axis=2)
    whole = jnp.concatenate([low, high], axis=1)
    return whole.reshape(whole.shape[0] * CELLS, FACE)


def neighbours(parts, step):
    shape = parts[0].shape
    x = iota(shape, 1)
    lane = iota(shape, 2)
    y = lane >> 4
    z = lane & 15

    sums = []
    ys_up = [roll(v, 16 * step, 2) for v in parts]
    ys_down = ys_up if step == 4 else [roll(v, -16 * step, 2) for v in parts]
    xs_up = [roll(v, step, 1) for v in parts]
    xs_down = xs_up if step == 4 else [roll(v, -step, 1) for v in parts]
    for i in (0, 1):
        for j in (0, 1):
            k = 2 * i + j
            v = parts[k]
            total = jnp.where(z >= step, roll(v, step, 2), 0.0)
            total = total + jnp.where(z < CELLS - step, roll(v, -step, 2), 0.0)
            before = ys_up[k - 1] if j == 1 else 0.0
            total = total + jnp.where(y >= step, ys_up[k], before)
            after = ys_down[k + 1] if j == 0 else 0.0
            total = total + jnp.where(y < 8 - step, ys_down[k], after)
            before = xs_up[k - 2] if i == 1 else 0.0
            total = total + jnp.where(x >= step, xs_up[k], before)
            after = xs_down[k + 2] if i == 0 else 0.0
            total = total + jnp.where(x < 8 - step, xs_down[k], after)
            sums.append(total)
    return sums


def block_mean(parts, step):
    shape = parts[0].shape
    x = iota(shape, 1)
    lane = iota(shape, 2)

    def pair(v, by, axis, even):
        count = v.shape[axis]
        return v + jnp.where(even, pltpu.roll(v, count - by, axis), pltpu.roll(v, by, axis))

    result = []
    for v in parts:
        v = pair(v, step, 2, (lane & step) == 0)
        v = pair(v, 16 * step, 2, ((lane >> 4) & step) == 0)
        v = pair(v, step, 1, (x & step) == 0)
        result.append(v * 0.125)
    return result


def merge_mean(parts):
    lane = iota((8, 128), 1)
    odd_z, odd_y = (lane & 1) == 1, ((lane >> 4) & 1) == 1
    even_x = (iota((8, 128), 0) & 1) == 0
    result = []
    for v in parts:
        a = v[0] + roll(v[0], -1, 1)
        b = v[1] + roll(v[1], 1, 1)
        c = v[2] + roll(v[2], -1, 1)
        a, b, c = a + roll(a, -16, 1), b + roll(b, -16, 1), c + roll(c, 16, 1)
        m = jnp.where(odd_y, c, jnp.where(odd_z, b, a))
        m = m + jnp.where(even_x, roll(m, -1, 0), roll(m, 1, 0))
        result.append((m * 0.125)[None])
    return result


def unmerge(parts):
    lane = iota((8, 128), 1)
    odd_z, odd_y = (lane & 1) == 1, ((lane >> 4) & 1) == 1
    result = []
    for v in parts:
        v = v[0]
        even = jnp.where(odd_z, roll(v, 1, 1), v)
        odd = jnp.where(odd_z, v, roll(v, -1, 1))
        comps = [
            jnp.where(odd_y, roll(even, 16, 1), even),
            jnp.where(odd_y, roll(odd, 16, 1), odd),
            jnp.where(odd_y, even, roll(even, -16, 1)),
        ]
        result.append(jnp.stack(comps, axis=0))
    return result


def broad(parts):
    return [jnp.broadcast_to(v, (3,) + v.shape[1:]) for v in parts]


def coarse_weights(scale2):
    shape = scale2[0].shape
    x = iota(shape, 1)
    y = iota(shape, 2) >> 4
    z = iota(shape, 2) & 15
    result = []
    for k, w in enumerate(scale2):
        near = w * 0.0625
        other_y = flag(y < 4) if k & 1 else flag(y >= 4)
        other_x = flag(x < 4) if k & 2 else flag(x >= 4)
        result.append((near, near * flag(z >= 4), near * flag(z < 12), near * other_y, near * other_x))
    return result


def coarse_solve(source, scale2, weights):
    wb = [w * s for w, s in zip(scale2, source)]
    v = wb
    for _ in range(COARSE_SWEEPS - 1):
        along_y = [roll(a, 64, 2) for a in v]
        along_x = [roll(a, 4, 1) for a in v]
        new = []
        for k, (near, low, high, other_y, other_x) in enumerate(weights):
            total = (KEEP * v[k] + wb[k]) + near * (along_y[k] + along_x[k])
            total = total + (other_y * along_y[k ^ 1] + other_x * along_x[k ^ 2])
            new.append(total + (low * roll(v[k], 4, 2) + high * roll(v[k], -4, 2)))
        v = new
    return v


def middle_solve(source, scale1, scale2, weights, meanwhile):
    wb = [w * s for w, s in zip(scale1, source)]
    near = neighbours(wb, 2)
    remain = [KEEP * s + 0.25 * n for s, n in zip(source, near)]
    coarse = coarse_solve(block_mean(remain, 2), scale2, weights)
    v = [a + c for a, c in zip(wb, coarse)]
    near = neighbours(v, 2)
    return unmerge([KEEP * a + (c + (w * 0.25) * n) for a, c, w, n in zip(v, wb, scale1, near)])


def local_solve(source, diag0, scale0, scale1, scale2, weights, meanwhile):
    wb = [w * s for w, s in zip(scale0, source)]
    v = None
    for cycle in range(2):
        if cycle == 0:
            v = wb
            remain = [KEEP * s + n for s, n in zip(source, neighbours(v, 1))]
        else:
            near = neighbours(v, 1)
            v = [KEEP * a + (c + w * n) for a, c, w, n in zip(v, wb, scale0, near)]
            near = neighbours(v, 1)
            remain = [(s - d * a) + n for s, d, a, n in zip(source, diag0, v, near)]
        hook = meanwhile if cycle else lambda: None
        coarse = middle_solve(merge_mean(remain), scale1, scale2, weights, hook)
        v = [a + c for a, c in zip(v, coarse)]
        hook()
        near = neighbours(v, 1)
        v = [KEEP * a + (c + w * n) for a, c, w, n in zip(v, wb, scale0, near)]
    return v


def exact_dot(left, right):
    high = left.astype(BF16)
    rest = left - high.astype(F32)
    mid = rest.astype(BF16)
    low = (rest - mid.astype(F32)).astype(BF16)
    whole = jnp.dot(jnp.concatenate([high, mid, low], axis=0), right, preferred_element_type=F32)
    n = left.shape[0]
    return whole[:n] + (whole[n : 2 * n] + whole[2 * n :])


def spread(rows):
    own = (iota((8, 128), 1) >> 4) == iota((8, 128), 0)
    tiles = [jnp.where(own, jnp.broadcast_to(r[:, h : h + 128], (8, 128)), 0.0) for r in rows for h in (0, 128)]
    return jnp.concatenate(tiles, axis=0)


def collect(field):
    own = (iota((8, 128), 1) >> 4) == iota((8, 128), 0)
    tiles = [
        jnp.sum(jnp.where(own, field[8 * i : 8 * i + 8], 0.0), axis=0, keepdims=True) for i in range(6)
    ]
    return [jnp.concatenate(tiles[2 * c : 2 * c + 2], axis=1) for c in range(3)]


def kernel(
    n_region,
    n_sub,
    direction,
    residual,
    reaction,
    viscosity,
    primal_index,
    region_inverse,
    coarse_map,
    global_inverse,
    jump,
    alpha,
    velocity,
    pressure,
    v_dir,
    v_res,
    v_react,
    v_visc,
    v_index,
    v_rows,
    v_map,
    v_ginv,
    table_y,
    table_z,
    table_back,
    padded_index,
    halo,
    face_send,
    after,
    packet,
    gather_y,
    gather,
    block_sums,
    gather_sums,
    packet2,
    gather2,
    packet3,
    gather3,
    sent_rows,
    load_sem,
    halo_send,
    halo_recv,
    back_send,
    back_recv,
    sum_send,
    sum_recv,
):
    region = lax.axis_index("region")
    sub = lax.axis_index("sub")

    n_y = n_sub // Z_LINE
    at_y = sub >> (Z_LINE.bit_length() - 1)
    at_z = sub & (Z_LINE - 1)

    def sub_peer(i):
        return (region, (sub + i) & (n_sub - 1))

    def region_peer(i):
        return ((region + i) & (n_region - 1), sub)

    def y_peer(i):
        return (region, ((at_y + i) & (n_y - 1)) * Z_LINE + at_z)

    def z_peer(i):
        return (region, at_y * Z_LINE + ((at_z + i) & (Z_LINE - 1)))

    loads = [
        pltpu.make_async_copy(src, dst, load_sem.at[i])
        for i, (src, dst) in enumerate(
            (
                (direction, v_dir),
                (primal_index, v_index),
                (coarse_map, v_map),
                (residual, v_res),
                (reaction, v_react),
                (region_inverse, v_rows),
                (global_inverse, v_ginv),
                (viscosity, v_visc),
            )
        )
    ]
    for load in loads:
        load.start()

    barrier = pltpu.get_barrier_semaphore()

    def hops_of(i):
        carry = [min(j, n_y - j) for j in (i // Z_LINE, (i // Z_LINE + 1) % n_y)]
        return max(carry) + min(i % Z_LINE, Z_LINE - i % Z_LINE)

    urgent = [n_sub - DOM_Z, n_sub - 1, DOM_Z, 1]
    others = sorted((i for i in range(1, n_sub) if i not in urgent), key=lambda i: -hops_of(i))
    near = [sub_peer(i) for i in urgent] + [region_peer(n_region - 1), region_peer(1)]
    on_sub = [sub_peer(i) for i in others + urgent]
    near += [sub_peer(i) for i in others] + [region_peer(i) for i in range(2, n_region - 1)]
    for peer in near:
        pl.semaphore_signal(barrier, inc=1, device_id=peer, device_id_type=MESH)

    def send_all(src, dst_of_me, peers, index):
        for peer in peers:
            pltpu.make_async_remote_copy(
                src_ref=src,
                dst_ref=dst_of_me,
                send_sem=sum_send.at[index],
                recv_sem=sum_recv.at[index],
                device_id=peer,
                device_id_type=MESH,
            ).start()

    def all_of(buffer, peers, index):
        part = buffer.at[pl.ds(0, len(peers))] if peers else buffer
        return pltpu.make_async_remote_copy(
            src_ref=part,
            dst_ref=part,
            send_sem=sum_send.at[index],
            recv_sem=sum_recv.at[index],
            device_id=(peers or on_y)[0],
            device_id_type=MESH,
        )

    on_y = [y_peer(i) for i in range(1, n_y)]
    on_z = [z_peer(i) for i in range(1, Z_LINE)]
    on_region = [region_peer(i) for i in range(1, n_region)]

    at_x = region >> 1
    at_c = region & 1
    n_x = n_region // 2
    found = []
    for dx in range(n_x):
        for dc in range(2):
            for dy in range(n_y):
                for dz in range(Z_LINE):
                    if dx or dc or dy or dz:
                        hops = min(dx, n_x - dx) + min(dy, n_y - dy) + min(dz, Z_LINE - dz)
                        found.append((-hops, dx, dc, dy, dz))
    found.sort()
    xs = [((at_x + i) & (n_x - 1)) * 2 for i in range(n_x)]
    cs = [(at_c + i) & 1 for i in range(2)]
    ys = [((at_y + i) & (n_y - 1)) * Z_LINE for i in range(n_y)]
    zs = [((at_z + i) & (Z_LINE - 1)) for i in range(Z_LINE)]
    everyone = [(xs[dx] + cs[dc], ys[dy] + zs[dz]) for _, dx, dc, dy, dz in found]

    loads[0].wait()
    loads[1].wait()
    padded_index[...] = jnp.full((8, 128), -1, jnp.int32)
    padded_index[0:1, 0:96] = v_index[...]
    index_row = padded_index[0:1, :]
    index_col = jnp.transpose(jnp.broadcast_to(index_row.astype(F32), (128, 128))).astype(jnp.int32)
    lane128 = iota((128, 128), 1)
    hit = jnp.where((index_col & 127) == lane128, 1.0, 0.0)
    key_col = index_col >> 7
    picked = jnp.zeros((128, 128), F32)
    for d in range(3):
        for c in range(3):
            for h in range(2):
                r = (d * 3 + c) * 2 + h
                values = v_dir[d, c, :, 128 * h : 128 * h + 128]
                picked = jnp.where(key_col == r, jnp.broadcast_to(values, (128, 128)), picked)
    picked = picked * hit
    primal_row = jnp.sum(jnp.transpose(picked), axis=0, keepdims=True)
    primal_col = jnp.sum(picked, axis=1, keepdims=True)[:96]
    loads[2].wait()
    share = jnp.sum(primal_col * v_map[0], axis=0, keepdims=True)
    loads[3].wait()
    squares = jnp.sum(v_res[...] * v_res[...])
    lane_row = iota((1, 128), 1)
    packet[0:1, :] = jnp.where(lane_row < 96, primal_row, squares)
    for j in range(3):
        packet[j + 1 : j + 2, :] = share[:, 128 * j : 128 * j + 128]
    gather_y[at_y] = packet[...]
    gather[sub] = packet[0:1, :]

    pl.semaphore_wait(barrier, len(near))

    def face_copy(src, dst, send, recv, peer):
        return pltpu.make_async_remote_copy(
            src_ref=src, dst_ref=dst, send_sem=send, recv_sem=recv, device_id=peer, device_id_type=MESH
        )

    below = (region_peer(n_region - 1), sub_peer(n_sub - DOM_Z), sub_peer(n_sub - 1))
    faces = [
        face_copy(v_dir.at[1], halo.at[1], halo_send.at[0], halo_recv.at[0], sub_peer(DOM_Z)),
        face_copy(v_dir.at[2], halo.at[2], halo_send.at[0], halo_recv.at[0], sub_peer(1)),
        face_copy(v_dir.at[0], halo.at[0], halo_send.at[0], halo_recv.at[0], region_peer(1)),
    ]
    for copy in faces:
        copy.start()
    send_all(packet.at[pl.ds(0, 1)], gather.at[sub], on_sub, 1)
    send_all(packet, gather_y.at[at_y], on_y, 0)
    row_i = iota((128, FACE), 0)
    col_i = iota((128, FACE), 1)
    to_y = jnp.where((row_i[:, :128] & 15) == (col_i[:, :128] & 15), 1.0, 0.0).astype(BF16)
    to_z = jnp.where((row_i & 15) == (col_i >> 4), 1.0, 0.0).astype(BF16)
    table_y[...] = to_y
    table_z[...] = to_z
    row_i = iota((FACE, 128), 0)
    col_i = iota((FACE, 128), 1)
    table_back[...] = jnp.where((row_i >> 4) == (col_i & 15), 1.0, 0.0).astype(BF16)
    lane = iota((CELLS, FACE), 1)
    y_lane = lane >> 4
    z_lane = lane & 15
    x_row = iota((CELLS, FACE), 0)

    def tile3(mask):
        return jnp.concatenate([mask] * 3, axis=0)

    def natural(face_rows, edge):
        in_y = exact_dot(spread(face_rows[1]), table_y[...])
        in_z = exact_dot(spread(face_rows[2]), table_z[...])
        blocks = []
        for c in range(3):
            rows = slice(CELLS * c, CELLS * c + CELLS)
            both = jnp.concatenate([in_y[rows], in_y[rows]], axis=1)
            part = jnp.where(x_row == edge, jnp.broadcast_to(face_rows[0][c], (CELLS, FACE)), 0.0)
            part = part + jnp.where(y_lane == edge, both, 0.0)
            part = part + jnp.where(z_lane == edge, in_z[rows], 0.0)
            blocks.append(part)
        return jnp.concatenate(blocks, axis=0)

    upper = CELLS - 1
    own_faces = natural([[v_dir[d, c] for c in range(3)] for d in range(3)], upper)
    loads[4].wait()
    react0 = split(v_react[0])
    react1 = block_mean(react0, 1)
    react2 = block_mean(react1, 2)
    diag0 = broad([r + 6.0 for r in react0])
    scale0 = broad([DAMPING / (r + 6.0) for r in react0])
    scale1 = [DAMPING / (r + 6.0 * 0.25) for r in react1]
    scale2 = [DAMPING / (r + 6.0 * 0.0625) for r in react2]
    weights = coarse_weights(scale2)

    all_of(gather_y, on_y, 0).wait_recv()
    summed = jnp.sum(gather_y[...], axis=0)
    block_sums[0:3, :] = summed[1:4]
    block_sums[3:4, :] = summed[0:1]
    gather_sums[at_z] = block_sums[...]
    send_all(block_sums, gather_sums.at[at_z], on_z, 4)

    def lane_total(v):
        tall = jnp.concatenate([v, jnp.zeros((32, 128), F32)], axis=0)
        return jnp.sum(jnp.transpose(tall), axis=0, keepdims=True)

    region_lanes = []

    def region_operator():
        all_of(gather, on_sub, 1).wait_recv()
        loads[5].wait()
        rows_y = n_sub // DOM_Z
        lane_a = iota((rows_y, 128), 1)
        quads = []
        for b in range(DOM_Z):
            quads.append(jnp.concatenate([gather[DOM_Z * a + b] for a in range(rows_y)], axis=0))

        def shifted(v, by):
            return pltpu.roll(v, by % 128, 1) if by % 128 else v

        packed = [
            jnp.where(lane_a < 96, quads[0], shifted(quads[1], 96)),
            jnp.where(lane_a < 64, shifted(quads[1], -32), shifted(quads[2], 64)),
            jnp.where(lane_a < 32, shifted(quads[2], -64), shifted(quads[3], 32)),
        ]
        lanes = jnp.zeros((96, 128), F32)
        for a in range(rows_y):
            for j in range(3):
                at = (3 * a + j) * 128
                lanes = lanes + v_rows[0, :, at : at + 128] * packed[j][a : a + 1, :]

        region_lanes.append(lanes)

    all_faces = face_copy(halo, halo, halo_send.at[0], halo_recv.at[0], sub_peer(1))
    all_faces.wait_recv()
    under = natural([[halo[d, c] for c in range(3)] for d in range(3)], 0)
    source = own_faces - under
    base = join(local_solve(split(source), diag0, scale0, scale1, scale2, weights, region_operator))

    part = jnp.sum(source * base, axis=0, keepdims=True)
    part = part[:, :128] + part[:, 128:] + jnp.sum(primal_col * region_lanes[0], axis=0, keepdims=True)
    packet3[...] = part
    place = region * n_sub + sub
    mine = gather3.at[place >> 3, pl.ds(place & 7, 1)]
    send_all(packet3, mine, everyone[:46], 3)
    pltpu.make_async_copy(packet3, mine, sum_recv.at[3]).start()

    def extract(edge):
        half = 128 if edge else 0
        at_edge = (iota((3 * CELLS, 128), 1) >> 4) == (edge & 7)
        in_y = collect(exact_dot(jnp.where(at_edge, base[:, half : half + 128], 0.0), table_y[...]))
        in_z = collect(exact_dot(jnp.where(tile3(z_lane == edge), base, 0.0), table_back[...]))
        in_x = [base[CELLS * c + edge : CELLS * c + edge + 1] for c in range(3)]
        return [in_x, in_y, in_z]

    lower_rows = extract(0)
    for d in range(3):
        for c in range(3):
            face_send[d, c] = lower_rows[d][c]
    backs = [
        pltpu.make_async_remote_copy(
            src_ref=face_send.at[d],
            dst_ref=after.at[d],
            send_sem=back_send.at[0],
            recv_sem=back_recv.at[0],
            device_id=below[d],
            device_id_type=MESH,
        )
        for d in (1, 2, 0)
    ]
    for copy in backs:
        copy.start()

    send_all(packet3, mine, everyone[46:158], 3)

    all_of(gather_sums, on_z, 4).wait_recv()
    packet2[...] = jnp.sum(gather_sums[...], axis=0)
    gather2[region] = packet2[...]
    send_all(packet2, gather2.at[region], on_region, 2)

    send_all(packet3, mine, everyone[158:], 3)

    all_of(gather2, on_region, 2).wait_recv()
    whole = jnp.sum(gather2[...], axis=0)
    squares_all = jnp.sum(jnp.where(lane_row == 96, whole[3:4, :], 0.0))
    total = jnp.concatenate([whole[0:1, :], whole[1:2, :], whole[2:3, :]], axis=1)
    loads[6].wait()
    top = lax.dot_general(
        jnp.broadcast_to(total, (8, 384)),
        v_ginv[...],
        (((1,), (1,)), ((), ())),
        precision=lax.Precision.HIGHEST,
        preferred_element_type=F32,
    )[0:1]
    energy = jnp.sum(total * top)
    weighted = v_map[0] * top
    lanes = weighted[:, :128] + weighted[:, 128:256] + weighted[:, 256:]
    lifted = lane_total(region_lanes[0] + lanes)
    key_row = jnp.broadcast_to(index_row >> 7, (32, 128))
    placed = jnp.where(key_row == iota((32, 128), 0), jnp.broadcast_to(lifted, (32, 128)), 0.0)
    placed = exact_dot(placed, hit.astype(BF16))

    def lifted_row(d, c):
        r = (d * 3 + c) * 2
        return jnp.concatenate([placed[r : r + 1], placed[r + 1 : r + 2]], axis=1)

    lifted_rows = [[lifted_row(d, c) for c in range(3)] for d in range(3)]
    field = base + natural(lifted_rows, upper)
    upper_rows = extract(upper)
    for c in range(3):
        velocity[0, c] = field[CELLS * c : CELLS * c + CELLS]

    all_backs = face_copy(after, after, back_send.at[0], back_recv.at[0], sub_peer(1))
    all_backs.wait_recv()
    loads[7].wait()
    v = [field[CELLS * c : CELLS * c + CELLS] for c in range(3)]
    edge_x = jnp.broadcast_to(after[0, 0], (CELLS, FACE))
    edge_y = exact_dot(spread([after[1, 1]]), table_y[...])
    edge_y = jnp.concatenate([edge_y, edge_y], axis=1)
    edge_z = exact_dot(spread([after[2, 2]]), table_z[...])
    step_x = jnp.where(x_row == upper, edge_x, pltpu.roll(v[0], CELLS - 1, 0)) - v[0]
    step_y = jnp.where(y_lane == upper, edge_y, pltpu.roll(v[1], FACE - CELLS, 1)) - v[1]
    step_z = jnp.where(z_lane == upper, edge_z, pltpu.roll(v[2], FACE - 1, 1)) - v[2]
    pressure[0] = -v_visc[0] * (step_x + step_y + step_z)
    for d in range(3):
        for c in range(3):
            jump[d, c] = upper_rows[d][c] + lifted_rows[d][c] - after[d, c]

    all_of(gather3, None, 3).wait_recv()
    curvature = jnp.sum(gather3[...]) + energy
    alpha[...] = jnp.broadcast_to(squares_all / curvature, (8, 128))

    all_faces.wait_send()
    all_backs.wait_send()
    all_of(gather_y, on_y, 0).wait_send()
    all_of(gather, on_sub, 1).wait_send()
    all_of(gather_sums, on_z, 4).wait_send()
    all_of(gather2, on_region, 2).wait_send()
    all_of(sent_rows, None, 3).wait_send()


def finish(multipliers, direction, residual, jump, alpha, velocity, pressure, *outs):
    step = jnp.broadcast_to(alpha[0:1, 0:1], (1, FACE))
    for d in range(3):
        for c in range(3):
            outs[0][d, c] = multipliers[d, c] + step * direction[d, c]
            outs[1][d, c] = residual[d, c] - step * jump[d, c]
    outs[2][...] = velocity[...]
    outs[3][...] = pressure[...]


def solution(mesh):
    n_region = mesh.shape["region"]
    n_sub = mesh.shape["sub"]

    def body(multipliers, direction, residual, *rest):
        faces = [a.reshape(3, 3, 1, FACE) for a in (multipliers, direction, residual)]
        args = [pltpu.with_memory_space_constraint(a, pltpu.HBM) for a in (faces[1], faces[2]) + rest]
        face = jax.ShapeDtypeStruct((3, 3, 1, FACE), F32)
        cells = jax.ShapeDtypeStruct((1, 3, CELLS, FACE), F32)
        scalar_cells = jax.ShapeDtypeStruct((1, CELLS, FACE), F32)
        inner = pl.pallas_call(
            functools.partial(kernel, n_region, n_sub),
            out_shape=[face, jax.ShapeDtypeStruct((8, 128), F32), cells, scalar_cells],
            in_specs=[pl.BlockSpec(memory_space=pltpu.HBM)] * 8,
            out_specs=[pl.BlockSpec(memory_space=pltpu.VMEM)] * 4,
            scratch_shapes=[pltpu.VMEM(a.shape, a.dtype) for a in args]
            + [
                pltpu.VMEM((128, 128), BF16),
                pltpu.VMEM((128, FACE), BF16),
                pltpu.VMEM((FACE, 128), BF16),
                pltpu.VMEM((8, 128), jnp.int32),
                pltpu.VMEM((3, 3, 1, FACE), F32),
                pltpu.VMEM((3, 3, 1, FACE), F32),
                pltpu.VMEM((3, 3, 1, FACE), F32),
                pltpu.VMEM((4, 128), F32),
                pltpu.VMEM((n_sub // Z_LINE, 4, 128), F32),
                pltpu.VMEM((n_sub, 1, 128), F32),
                pltpu.VMEM((4, 128), F32),
                pltpu.VMEM((Z_LINE, 4, 128), F32),
                pltpu.VMEM((4, 128), F32),
                pltpu.VMEM((n_region, 4, 128), F32),
                pltpu.VMEM((1, 128), F32),
                pltpu.VMEM((n_region * n_sub // 8, 8, 128), F32),
                pltpu.VMEM((n_region * n_sub - 1, 1, 128), F32),
                pltpu.SemaphoreType.DMA((8,)),
                pltpu.SemaphoreType.DMA((1,)),
                pltpu.SemaphoreType.DMA((1,)),
                pltpu.SemaphoreType.DMA((1,)),
                pltpu.SemaphoreType.DMA((1,)),
                pltpu.SemaphoreType.DMA((5,)),
                pltpu.SemaphoreType.DMA((5,)),
            ],
            compiler_params=pltpu.CompilerParams(
                collective_id=0, has_side_effects=True, vmem_limit_bytes=VMEM_LIMIT
            ),
            name="feti",
        )
        jump, alpha, velocity, pressure = inner(*args)
        outs = pl.pallas_call(
            finish,
            out_shape=[face, face, cells, scalar_cells],
            in_specs=[pl.BlockSpec(memory_space=pltpu.VMEM)] * 7,
            out_specs=[pl.BlockSpec(memory_space=pltpu.VMEM)] * 4,
            compiler_params=pltpu.CompilerParams(vmem_limit_bytes=VMEM_LIMIT),
            name="finish",
        )(*faces, jump, alpha, velocity, pressure)
        shape = multipliers.shape
        return outs[0].reshape(shape), outs[1].reshape(shape), outs[2], outs[3]

    in_specs = (
        P(("region", "sub"), None, None, None),
        P(("region", "sub"), None, None, None),
        P(("region", "sub"), None, None, None),
        P(("region", "sub"), None, None),
        P(("region", "sub"), None, None),
        P(("region", "sub"), None),
        P("region", "sub", None),
        P(("region", "sub"), None, None),
        P(),
    )
    out_specs = (
        P(("region", "sub"), None, None, None),
        P(("region", "sub"), None, None, None),
        P(("region", "sub"), None, None, None),
        P(("region", "sub"), None, None),
    )
    return jax.shard_map(body, mesh=mesh, in_specs=in_specs, out_specs=out_specs, check_vma=False)
```

```python
import functools

import jax
import jax.numpy as jnp
from jax import lax
from jax.experimental import pallas as pl
from jax.experimental.pallas import tpu as pltpu
from jax.sharding import PartitionSpec as P

DOM_Z = 4
Z_LINE = 8
COARSE_SWEEPS = 8
CELLS = 16
FACE = 256
DAMPING = 0.8
VMEM_LIMIT = 16 * 1024 * 1024
KEEP = 0.2
MESH = pl.DeviceIdType.MESH
F32 = jnp.float32
BF16 = jnp.bfloat16


def roll(v, by, axis):
    return pltpu.roll(v, by % v.shape[axis], axis)


def flag(condition):
    return jnp.where(condition, 1.0, 0.0)


def iota(shape, axis):
    return lax.broadcasted_iota(jnp.int32, shape, axis)


def split(field):
    lead = field.shape[0] // CELLS
    cubic = field.reshape(lead, CELLS, FACE)
    return [cubic[:, 8 * i : 8 * i + 8, 128 * j : 128 * j + 128] for i in (0, 1) for j in (0, 1)]


def join(parts):
    low = jnp.concatenate([parts[0], parts[1]], axis=2)
    high = jnp.concatenate([parts[2], parts[3]], axis=2)
    whole = jnp.concatenate([low, high], axis=1)
    return whole.reshape(whole.shape[0] * CELLS, FACE)


def neighbours(parts, step):
    shape = parts[0].shape
    x = iota(shape, 1)
    lane = iota(shape, 2)
    y = lane >> 4
    z = lane & 15

    sums = []
    ys_up = [roll(v, 16 * step, 2) for v in parts]
    ys_down = ys_up if step == 4 else [roll(v, -16 * step, 2) for v in parts]
    xs_up = [roll(v, step, 1) for v in parts]
    xs_down = xs_up if step == 4 else [roll(v, -step, 1) for v in parts]
    for i in (0, 1):
        for j in (0, 1):
            k = 2 * i + j
            v = parts[k]
            total = jnp.where(z >= step, roll(v, step, 2), 0.0)
            total = total + jnp.where(z < CELLS - step, roll(v, -step, 2), 0.0)
            before = ys_up[k - 1] if j == 1 else 0.0
            total = total + jnp.where(y >= step, ys_up[k], before)
            after = ys_down[k + 1] if j == 0 else 0.0
            total = total + jnp.where(y < 8 - step, ys_down[k], after)
            before = xs_up[k - 2] if i == 1 else 0.0
            total = total + jnp.where(x >= step, xs_up[k], before)
            after = xs_down[k + 2] if i == 0 else 0.0
            total = total + jnp.where(x < 8 - step, xs_down[k], after)
            sums.append(total)
    return sums


def block_mean(parts, step):
    shape = parts[0].shape
    x = iota(shape, 1)
    lane = iota(shape, 2)

    def pair(v, by, axis, even):
        count = v.shape[axis]
        return v + jnp.where(even, pltpu.roll(v, count - by, axis), pltpu.roll(v, by, axis))

    result = []
    for v in parts:
        v = pair(v, step, 2, (lane & step) == 0)
        v = pair(v, 16 * step, 2, ((lane >> 4) & step) == 0)
        v = pair(v, step, 1, (x & step) == 0)
        result.append(v * 0.125)
    return result


def merge_mean(parts):
    lane = iota((8, 128), 1)
    odd_z, odd_y = (lane & 1) == 1, ((lane >> 4) & 1) == 1
    even_x = (iota((8, 128), 0) & 1) == 0
    result = []
    for v in parts:
        a = v[0] + roll(v[0], -1, 1)
        b = v[1] + roll(v[1], 1, 1)
        c = v[2] + roll(v[2], -1, 1)
        a, b, c = a + roll(a, -16, 1), b + roll(b, -16, 1), c + roll(c, 16, 1)
        m = jnp.where(odd_y, c, jnp.where(odd_z, b, a))
        m = m + jnp.where(even_x, roll(m, -1, 0), roll(m, 1, 0))
        result.append((m * 0.125)[None])
    return result


def unmerge(parts):
    lane = iota((8, 128), 1)
    odd_z, odd_y = (lane & 1) == 1, ((lane >> 4) & 1) == 1
    result = []
    for v in parts:
        v = v[0]
        even = jnp.where(odd_z, roll(v, 1, 1), v)
        odd = jnp.where(odd_z, v, roll(v, -1, 1))
        comps = [
            jnp.where(odd_y, roll(even, 16, 1), even),
            jnp.where(odd_y, roll(odd, 16, 1), odd),
            jnp.where(odd_y, even, roll(even, -16, 1)),
        ]
        result.append(jnp.stack(comps, axis=0))
    return result


def broad(parts):
    return [jnp.broadcast_to(v, (3,) + v.shape[1:]) for v in parts]


def coarse_weights(scale2):
    shape = scale2[0].shape
    x = iota(shape, 1)
    y = iota(shape, 2) >> 4
    z = iota(shape, 2) & 15
    result = []
    for k, w in enumerate(scale2):
        near = w * 0.0625
        other_y = flag(y < 4) if k & 1 else flag(y >= 4)
        other_x = flag(x < 4) if k & 2 else flag(x >= 4)
        result.append((near, near * flag(z >= 4), near * flag(z < 12), near * other_y, near * other_x))
    return result


def coarse_solve(source, scale2, weights):
    wb = [w * s for w, s in zip(scale2, source)]
    v = wb
    for _ in range(COARSE_SWEEPS - 1):
        along_y = [roll(a, 64, 2) for a in v]
        along_x = [roll(a, 4, 1) for a in v]
        new = []
        for k, (near, low, high, other_y, other_x) in enumerate(weights):
            total = (KEEP * v[k] + wb[k]) + near * (along_y[k] + along_x[k])
            total = total + (other_y * along_y[k ^ 1] + other_x * along_x[k ^ 2])
            new.append(total + (low * roll(v[k], 4, 2) + high * roll(v[k], -4, 2)))
        v = new
    return v


def middle_solve(source, scale1, scale2, weights, meanwhile):
    wb = [w * s for w, s in zip(scale1, source)]
    near = neighbours(wb, 2)
    remain = [KEEP * s + 0.25 * n for s, n in zip(source, near)]
    coarse = coarse_solve(block_mean(remain, 2), scale2, weights)
    v = [a + c for a, c in zip(wb, coarse)]
    near = neighbours(v, 2)
    return unmerge([KEEP * a + (c + (w * 0.25) * n) for a, c, w, n in zip(v, wb, scale1, near)])


def local_solve(source, diag0, scale0, scale1, scale2, weights, meanwhile):
    wb = [w * s for w, s in zip(scale0, source)]
    v = None
    for cycle in range(2):
        if cycle == 0:
            v = wb
            remain = [KEEP * s + n for s, n in zip(source, neighbours(v, 1))]
        else:
            near = neighbours(v, 1)
            v = [KEEP * a + (c + w * n) for a, c, w, n in zip(v, wb, scale0, near)]
            near = neighbours(v, 1)
            remain = [(s - d * a) + n for s, d, a, n in zip(source, diag0, v, near)]
        hook = meanwhile if cycle else lambda: None
        coarse = middle_solve(merge_mean(remain), scale1, scale2, weights, hook)
        v = [a + c for a, c in zip(v, coarse)]
        hook()
        near = neighbours(v, 1)
        v = [KEEP * a + (c + w * n) for a, c, w, n in zip(v, wb, scale0, near)]
    return v


def exact_dot(left, right):
    high = left.astype(BF16)
    rest = left - high.astype(F32)
    mid = rest.astype(BF16)
    low = (rest - mid.astype(F32)).astype(BF16)
    whole = jnp.dot(jnp.concatenate([high, mid, low], axis=0), right, preferred_element_type=F32)
    n = left.shape[0]
    return whole[:n] + (whole[n : 2 * n] + whole[2 * n :])


def spread(rows):
    own = (iota((8, 128), 1) >> 4) == iota((8, 128), 0)
    tiles = [jnp.where(own, jnp.broadcast_to(r[:, h : h + 128], (8, 128)), 0.0) for r in rows for h in (0, 128)]
    return jnp.concatenate(tiles, axis=0)


def collect(field):
    own = (iota((8, 128), 1) >> 4) == iota((8, 128), 0)
    tiles = [
        jnp.sum(jnp.where(own, field[8 * i : 8 * i + 8], 0.0), axis=0, keepdims=True) for i in range(6)
    ]
    return [jnp.concatenate(tiles[2 * c : 2 * c + 2], axis=1) for c in range(3)]


def kernel(
    n_region,
    n_sub,
    direction,
    residual,
    reaction,
    viscosity,
    primal_index,
    region_inverse,
    coarse_map,
    global_inverse,
    jump,
    alpha,
    velocity,
    pressure,
    v_dir,
    v_res,
    v_react,
    v_visc,
    v_index,
    v_rows,
    v_map,
    v_ginv,
    table_y,
    table_z,
    table_back,
    padded_index,
    halo,
    face_send,
    after,
    packet,
    gather_y,
    gather,
    block_sums,
    gather_sums,
    packet2,
    gather2,
    packet3,
    gather3,
    sent_rows,
    load_sem,
    halo_send,
    halo_recv,
    back_send,
    back_recv,
    sum_send,
    sum_recv,
):
    region = lax.axis_index("region")
    sub = lax.axis_index("sub")

    n_y = n_sub // Z_LINE
    at_y = sub >> (Z_LINE.bit_length() - 1)
    at_z = sub & (Z_LINE - 1)

    def sub_peer(i):
        return (region, (sub + i) & (n_sub - 1))

    def region_peer(i):
        return ((region + i) & (n_region - 1), sub)

    def y_peer(i):
        return (region, ((at_y + i) & (n_y - 1)) * Z_LINE + at_z)

    def z_peer(i):
        return (region, at_y * Z_LINE + ((at_z + i) & (Z_LINE - 1)))

    loads = [
        pltpu.make_async_copy(src, dst, load_sem.at[i])
        for i, (src, dst) in enumerate(
            (
                (direction, v_dir),
                (primal_index, v_index),
                (coarse_map, v_map),
                (residual, v_res),
                (reaction, v_react),
                (region_inverse, v_rows),
                (global_inverse, v_ginv),
                (viscosity, v_visc),
            )
        )
    ]
    for load in loads[:3]:
        load.start()

    barrier = pltpu.get_barrier_semaphore()

    def hops_of(i):
        carry = [min(j, n_y - j) for j in (i // Z_LINE, (i // Z_LINE + 1) % n_y)]
        return max(carry) + min(i % Z_LINE, Z_LINE - i % Z_LINE)

    urgent = [n_sub - DOM_Z, n_sub - 1, DOM_Z, 1]
    others = sorted((i for i in range(1, n_sub) if i not in urgent), key=lambda i: -hops_of(i))
    near = [sub_peer(i) for i in others[:2]] + [sub_peer(i) for i in urgent]
    near += [region_peer(n_region - 1), region_peer(1)]
    on_sub = [sub_peer(i) for i in others + urgent]
    near += [sub_peer(i) for i in others[2:]] + [region_peer(i) for i in range(2, n_region - 1)]
    for peer in near:
        pl.semaphore_signal(barrier, inc=1, device_id=peer, device_id_type=MESH)

    for load in loads[3:]:
        load.start()

    def send_all(src, dst_of_me, peers, index):
        for peer in peers:
            pltpu.make_async_remote_copy(
                src_ref=src,
                dst_ref=dst_of_me,
                send_sem=sum_send.at[index],
                recv_sem=sum_recv.at[index],
                device_id=peer,
                device_id_type=MESH,
            ).start()

    def all_of(buffer, peers, index):
        part = buffer.at[pl.ds(0, len(peers))] if peers else buffer
        return pltpu.make_async_remote_copy(
            src_ref=part,
            dst_ref=part,
            send_sem=sum_send.at[index],
            recv_sem=sum_recv.at[index],
            device_id=(peers or on_y)[0],
            device_id_type=MESH,
        )

    on_y = [y_peer(i) for i in range(1, n_y)]
    on_z = [z_peer(i) for i in range(1, Z_LINE)]
    on_region = [region_peer(i) for i in range(1, n_region)]

    at_x = region >> 1
    at_c = region & 1
    n_x = n_region // 2
    found = []
    for dx in range(n_x):
        for dc in range(2):
            for dy in range(n_y):
                for dz in range(Z_LINE):
                    if dx or dc or dy or dz:
                        hops = min(dx, n_x - dx) + min(dy, n_y - dy) + min(dz, Z_LINE - dz)
                        found.append((-hops, dx, dc, dy, dz))
    found.sort()
    xs = [((at_x + i) & (n_x - 1)) * 2 for i in range(n_x)]
    cs = [(at_c + i) & 1 for i in range(2)]
    ys = [((at_y + i) & (n_y - 1)) * Z_LINE for i in range(n_y)]
    zs = [((at_z + i) & (Z_LINE - 1)) for i in range(Z_LINE)]
    everyone = [(xs[dx] + cs[dc], ys[dy] + zs[dz]) for _, dx, dc, dy, dz in found]

    loads[0].wait()
    pl.semaphore_wait(barrier, len(near))

    def face_copy(src, dst, send, recv, peer):
        return pltpu.make_async_remote_copy(
            src_ref=src, dst_ref=dst, send_sem=send, recv_sem=recv, device_id=peer, device_id_type=MESH
        )

    below = (region_peer(n_region - 1), sub_peer(n_sub - DOM_Z), sub_peer(n_sub - 1))
    faces = [
        face_copy(v_dir.at[1], halo.at[1], halo_send.at[0], halo_recv.at[0], sub_peer(DOM_Z)),
        face_copy(v_dir.at[2], halo.at[2], halo_send.at[0], halo_recv.at[0], sub_peer(1)),
        face_copy(v_dir.at[0], halo.at[0], halo_send.at[0], halo_recv.at[0], region_peer(1)),
    ]
    for copy in faces:
        copy.start()
    loads[1].wait()
    padded_index[...] = jnp.full((8, 128), -1, jnp.int32)
    padded_index[0:1, 0:96] = v_index[...]
    index_row = padded_index[0:1, :]
    index_col = jnp.transpose(jnp.broadcast_to(index_row.astype(F32), (128, 128))).astype(jnp.int32)
    lane128 = iota((128, 128), 1)
    hit = jnp.where((index_col & 127) == lane128, 1.0, 0.0)
    key_col = index_col >> 7
    picked = jnp.zeros((128, 128), F32)
    for d in range(3):
        for c in range(3):
            for h in range(2):
                r = (d * 3 + c) * 2 + h
                values = v_dir[d, c, :, 128 * h : 128 * h + 128]
                picked = jnp.where(key_col == r, jnp.broadcast_to(values, (128, 128)), picked)
    picked = picked * hit
    primal_row = jnp.sum(jnp.transpose(picked), axis=0, keepdims=True)
    primal_col = jnp.sum(picked, axis=1, keepdims=True)[:96]
    loads[2].wait()
    share = jnp.sum(primal_col * v_map[0], axis=0, keepdims=True)
    loads[3].wait()
    squares = jnp.sum(v_res[...] * v_res[...])
    lane_row = iota((1, 128), 1)
    packet[0:1, :] = jnp.where(lane_row < 96, primal_row, squares)
    for j in range(3):
        packet[j + 1 : j + 2, :] = share[:, 128 * j : 128 * j + 128]
    gather_y[at_y] = packet[...]
    gather[sub] = packet[0:1, :]

    send_all(packet.at[pl.ds(0, 1)], gather.at[sub], on_sub, 1)
    send_all(packet, gather_y.at[at_y], on_y, 0)
    row_i = iota((128, FACE), 0)
    col_i = iota((128, FACE), 1)
    to_y = jnp.where((row_i[:, :128] & 15) == (col_i[:, :128] & 15), 1.0, 0.0).astype(BF16)
    to_z = jnp.where((row_i & 15) == (col_i >> 4), 1.0, 0.0).astype(BF16)
    table_y[...] = to_y
    table_z[...] = to_z
    row_i = iota((FACE, 128), 0)
    col_i = iota((FACE, 128), 1)
    table_back[...] = jnp.where((row_i >> 4) == (col_i & 15), 1.0, 0.0).astype(BF16)
    lane = iota((CELLS, FACE), 1)
    y_lane = lane >> 4
    z_lane = lane & 15
    x_row = iota((CELLS, FACE), 0)

    def tile3(mask):
        return jnp.concatenate([mask] * 3, axis=0)

    def natural(face_rows, edge):
        in_y = exact_dot(spread(face_rows[1]), table_y[...])
        in_z = exact_dot(spread(face_rows[2]), table_z[...])
        blocks = []
        for c in range(3):
            rows = slice(CELLS * c, CELLS * c + CELLS)
            both = jnp.concatenate([in_y[rows], in_y[rows]], axis=1)
            part = jnp.where(x_row == edge, jnp.broadcast_to(face_rows[0][c], (CELLS, FACE)), 0.0)
            part = part + jnp.where(y_lane == edge, both, 0.0)
            part = part + jnp.where(z_lane == edge, in_z[rows], 0.0)
            blocks.append(part)
        return jnp.concatenate(blocks, axis=0)

    upper = CELLS - 1
    own_faces = natural([[v_dir[d, c] for c in range(3)] for d in range(3)], upper)
    loads[4].wait()
    react0 = split(v_react[0])
    react1 = block_mean(react0, 1)
    react2 = block_mean(react1, 2)
    diag0 = broad([r + 6.0 for r in react0])
    scale0 = broad([DAMPING / (r + 6.0) for r in react0])
    scale1 = [DAMPING / (r + 6.0 * 0.25) for r in react1]
    scale2 = [DAMPING / (r + 6.0 * 0.0625) for r in react2]
    weights = coarse_weights(scale2)

    all_of(gather_y, on_y, 0).wait_recv()
    summed = jnp.sum(gather_y[...], axis=0)
    block_sums[0:3, :] = summed[1:4]
    block_sums[3:4, :] = summed[0:1]
    gather_sums[at_z] = block_sums[...]
    send_all(block_sums, gather_sums.at[at_z], on_z, 4)

    def lane_total(v):
        tall = jnp.concatenate([v, jnp.zeros((32, 128), F32)], axis=0)
        return jnp.sum(jnp.transpose(tall), axis=0, keepdims=True)

    region_lanes = []

    def region_operator():
        all_of(gather, on_sub, 1).wait_recv()
        loads[5].wait()
        rows_y = n_sub // DOM_Z
        lane_a = iota((rows_y, 128), 1)
        quads = []
        for b in range(DOM_Z):
            quads.append(jnp.concatenate([gather[DOM_Z * a + b] for a in range(rows_y)], axis=0))

        def shifted(v, by):
            return pltpu.roll(v, by % 128, 1) if by % 128 else v

        packed = [
            jnp.where(lane_a < 96, quads[0], shifted(quads[1], 96)),
            jnp.where(lane_a < 64, shifted(quads[1], -32), shifted(quads[2], 64)),
            jnp.where(lane_a < 32, shifted(quads[2], -64), shifted(quads[3], 32)),
        ]
        lanes = jnp.zeros((96, 128), F32)
        for a in range(rows_y):
            for j in range(3):
                at = (3 * a + j) * 128
                lanes = lanes + v_rows[0, :, at : at + 128] * packed[j][a : a + 1, :]

        region_lanes.append(lanes)

    all_faces = face_copy(halo, halo, halo_send.at[0], halo_recv.at[0], sub_peer(1))
    all_faces.wait_recv()
    under = natural([[halo[d, c] for c in range(3)] for d in range(3)], 0)
    source = own_faces - under
    base = join(local_solve(split(source), diag0, scale0, scale1, scale2, weights, region_operator))

    part = jnp.sum(source * base, axis=0, keepdims=True)
    part = part[:, :128] + part[:, 128:] + jnp.sum(primal_col * region_lanes[0], axis=0, keepdims=True)
    packet3[...] = part
    place = region * n_sub + sub
    mine = gather3.at[place >> 3, pl.ds(place & 7, 1)]
    send_all(packet3, mine, everyone[:46], 3)
    pltpu.make_async_copy(packet3, mine, sum_recv.at[3]).start()

    def extract(edge):
        half = 128 if edge else 0
        at_edge = (iota((3 * CELLS, 128), 1) >> 4) == (edge & 7)
        in_y = collect(exact_dot(jnp.where(at_edge, base[:, half : half + 128], 0.0), table_y[...]))
        in_z = collect(exact_dot(jnp.where(tile3(z_lane == edge), base, 0.0), table_back[...]))
        in_x = [base[CELLS * c + edge : CELLS * c + edge + 1] for c in range(3)]
        return [in_x, in_y, in_z]

    lower_rows = extract(0)
    for d in range(3):
        for c in range(3):
            face_send[d, c] = lower_rows[d][c]
    backs = [
        pltpu.make_async_remote_copy(
            src_ref=face_send.at[d],
            dst_ref=after.at[d],
            send_sem=back_send.at[0],
            recv_sem=back_recv.at[0],
            device_id=below[d],
            device_id_type=MESH,
        )
        for d in (1, 2, 0)
    ]
    for copy in backs:
        copy.start()

    send_all(packet3, mine, everyone[46:158], 3)

    all_of(gather_sums, on_z, 4).wait_recv()
    packet2[...] = jnp.sum(gather_sums[...], axis=0)
    gather2[region] = packet2[...]
    send_all(packet2, gather2.at[region], on_region, 2)

    send_all(packet3, mine, everyone[158:], 3)

    all_of(gather2, on_region, 2).wait_recv()
    whole = jnp.sum(gather2[...], axis=0)
    squares_all = jnp.sum(jnp.where(lane_row == 96, whole[3:4, :], 0.0))
    total = jnp.concatenate([whole[0:1, :], whole[1:2, :], whole[2:3, :]], axis=1)
    loads[6].wait()
    top = lax.dot_general(
        jnp.broadcast_to(total, (8, 384)),
        v_ginv[...],
        (((1,), (1,)), ((), ())),
        precision=lax.Precision.HIGHEST,
        preferred_element_type=F32,
    )[0:1]
    energy = jnp.sum(total * top)
    weighted = v_map[0] * top
    lanes = weighted[:, :128] + weighted[:, 128:256] + weighted[:, 256:]
    lifted = lane_total(region_lanes[0] + lanes)
    key_row = jnp.broadcast_to(index_row >> 7, (32, 128))
    placed = jnp.where(key_row == iota((32, 128), 0), jnp.broadcast_to(lifted, (32, 128)), 0.0)
    placed = exact_dot(placed, hit.astype(BF16))

    def lifted_row(d, c):
        r = (d * 3 + c) * 2
        return jnp.concatenate([placed[r : r + 1], placed[r + 1 : r + 2]], axis=1)

    lifted_rows = [[lifted_row(d, c) for c in range(3)] for d in range(3)]
    field = base + natural(lifted_rows, upper)
    upper_rows = extract(upper)
    for c in range(3):
        velocity[0, c] = field[CELLS * c : CELLS * c + CELLS]

    all_backs = face_copy(after, after, back_send.at[0], back_recv.at[0], sub_peer(1))
    all_backs.wait_recv()
    loads[7].wait()
    v = [field[CELLS * c : CELLS * c + CELLS] for c in range(3)]
    edge_x = jnp.broadcast_to(after[0, 0], (CELLS, FACE))
    edge_y = exact_dot(spread([after[1, 1]]), table_y[...])
    edge_y = jnp.concatenate([edge_y, edge_y], axis=1)
    edge_z = exact_dot(spread([after[2, 2]]), table_z[...])
    step_x = jnp.where(x_row == upper, edge_x, pltpu.roll(v[0], CELLS - 1, 0)) - v[0]
    step_y = jnp.where(y_lane == upper, edge_y, pltpu.roll(v[1], FACE - CELLS, 1)) - v[1]
    step_z = jnp.where(z_lane == upper, edge_z, pltpu.roll(v[2], FACE - 1, 1)) - v[2]
    pressure[0] = -v_visc[0] * (step_x + step_y + step_z)
    for d in range(3):
        for c in range(3):
            jump[d, c] = upper_rows[d][c] + lifted_rows[d][c] - after[d, c]

    all_of(gather3, None, 3).wait_recv()
    curvature = jnp.sum(gather3[...]) + energy
    alpha[...] = jnp.broadcast_to(squares_all / curvature, (8, 128))

    all_faces.wait_send()
    all_backs.wait_send()
    all_of(gather_y, on_y, 0).wait_send()
    all_of(gather, on_sub, 1).wait_send()
    all_of(gather_sums, on_z, 4).wait_send()
    all_of(gather2, on_region, 2).wait_send()
    all_of(sent_rows, None, 3).wait_send()


def finish(multipliers, direction, residual, jump, alpha, velocity, pressure, *outs):
    step = jnp.broadcast_to(alpha[0:1, 0:1], (1, FACE))
    for d in range(3):
        for c in range(3):
            outs[0][d, c] = multipliers[d, c] + step * direction[d, c]
            outs[1][d, c] = residual[d, c] - step * jump[d, c]
    outs[2][...] = velocity[...]
    outs[3][...] = pressure[...]


def solution(mesh):
    n_region = mesh.shape["region"]
    n_sub = mesh.shape["sub"]

    def body(multipliers, direction, residual, *rest):
        faces = [a.reshape(3, 3, 1, FACE) for a in (multipliers, direction, residual)]
        args = [pltpu.with_memory_space_constraint(a, pltpu.HBM) for a in (faces[1], faces[2]) + rest]
        face = jax.ShapeDtypeStruct((3, 3, 1, FACE), F32)
        cells = jax.ShapeDtypeStruct((1, 3, CELLS, FACE), F32)
        scalar_cells = jax.ShapeDtypeStruct((1, CELLS, FACE), F32)
        inner = pl.pallas_call(
            functools.partial(kernel, n_region, n_sub),
            out_shape=[face, jax.ShapeDtypeStruct((8, 128), F32), cells, scalar_cells],
            in_specs=[pl.BlockSpec(memory_space=pltpu.HBM)] * 8,
            out_specs=[pl.BlockSpec(memory_space=pltpu.VMEM)] * 4,
            scratch_shapes=[pltpu.VMEM(a.shape, a.dtype) for a in args]
            + [
                pltpu.VMEM((128, 128), BF16),
                pltpu.VMEM((128, FACE), BF16),
                pltpu.VMEM((FACE, 128), BF16),
                pltpu.VMEM((8, 128), jnp.int32),
                pltpu.VMEM((3, 3, 1, FACE), F32),
                pltpu.VMEM((3, 3, 1, FACE), F32),
                pltpu.VMEM((3, 3, 1, FACE), F32),
                pltpu.VMEM((4, 128), F32),
                pltpu.VMEM((n_sub // Z_LINE, 4, 128), F32),
                pltpu.VMEM((n_sub, 1, 128), F32),
                pltpu.VMEM((4, 128), F32),
                pltpu.VMEM((Z_LINE, 4, 128), F32),
                pltpu.VMEM((4, 128), F32),
                pltpu.VMEM((n_region, 4, 128), F32),
                pltpu.VMEM((1, 128), F32),
                pltpu.VMEM((n_region * n_sub // 8, 8, 128), F32),
                pltpu.VMEM((n_region * n_sub - 1, 1, 128), F32),
                pltpu.SemaphoreType.DMA((8,)),
                pltpu.SemaphoreType.DMA((1,)),
                pltpu.SemaphoreType.DMA((1,)),
                pltpu.SemaphoreType.DMA((1,)),
                pltpu.SemaphoreType.DMA((1,)),
                pltpu.SemaphoreType.DMA((5,)),
                pltpu.SemaphoreType.DMA((5,)),
            ],
            compiler_params=pltpu.CompilerParams(
                collective_id=0, has_side_effects=True, vmem_limit_bytes=VMEM_LIMIT
            ),
            name="feti",
        )
        jump, alpha, velocity, pressure = inner(*args)
        outs = pl.pallas_call(
            finish,
            out_shape=[face, face, cells, scalar_cells],
            in_specs=[pl.BlockSpec(memory_space=pltpu.VMEM)] * 7,
            out_specs=[pl.BlockSpec(memory_space=pltpu.VMEM)] * 4,
            compiler_params=pltpu.CompilerParams(vmem_limit_bytes=VMEM_LIMIT),
            name="finish",
        )(*faces, jump, alpha, velocity, pressure)
        shape = multipliers.shape
        return outs[0].reshape(shape), outs[1].reshape(shape), outs[2], outs[3]

    in_specs = (
        P(("region", "sub"), None, None, None),
        P(("region", "sub"), None, None, None),
        P(("region", "sub"), None, None, None),
        P(("region", "sub"), None, None),
        P(("region", "sub"), None, None),
        P(("region", "sub"), None),
        P("region", "sub", None),
        P(("region", "sub"), None, None),
        P(),
    )
    out_specs = (
        P(("region", "sub"), None, None, None),
        P(("region", "sub"), None, None, None),
        P(("region", "sub"), None, None, None),
        P(("region", "sub"), None, None),
    )
    return jax.shard_map(body, mesh=mesh, in_specs=in_specs, out_specs=out_specs, check_vma=False)
```
